32 devices in a mesh: row: 4 (over z), col: 8 (over y, x, core).
Axes of the slice: x: 2, y: 2, z: 4, core: 2. Of those that a mesh axis runs over, the one named last changes fastest.
Arguments:
- hidden: bfloat16 [4096, 2048], P(('row', 'col')), may hold values from -6 to 6
- cached_lengths: int32 [4], replicated, may hold values from 1024 to 4096, as said below
- request_order: int32 [4], replicated, may hold values from 0 to 3, each once
- cache_keys: bfloat16 [4, 4096, 2048], P('row', None, 'col'), may hold values from -480 to 480
- cache_values: bfloat16 [4, 4096, 2048], P('row', None, 'col'), may hold values from -6 to 6
- attn_gain: bfloat16 [2048], replicated, may hold values from 0.5 to 1.5
- w_qkv: bfloat16 [2048, 16, 384], P(None, 'col'), may hold values from -0.125 to 0.125
- w_out: bfloat16 [2048, 2048], P('col'), may hold values from -0.125 to 0.125
- moe_gain: bfloat16 [2048], replicated, may hold values from 0.5 to 1.5
- expert_ids: int32 [4096, 6], P(('row', 'col')), may hold values from 0 to 63, all different within a row; in each aligned block of 128 rows (0 to 127, 128 to 255, ...) at most 16 rows name the same one
- gate_weights: bfloat16 [4096, 6], P(('row', 'col')), may hold values from 0.049804688 to 0.3984375
- w_in: bfloat16 [128, 2048, 1408], P(('row', 'col')), may hold values from -0.125 to 0.125
- w_down: bfloat16 [128, 704, 2048], P(('row', 'col')), may hold values from -0.15625 to 0.15625
Outputs:
- new_hidden: bfloat16 [4096, 2048], P(('row', 'col'))
- new_keys: bfloat16 [4096, 2048], P('row', 'col')
- new_values: bfloat16 [4096, 2048], P('row', 'col')
The draws below stay inside these ranges and needn't reach their ends.
Inputs may be any that keep to these rules, and one draw needn't show every extreme that they name: `cached_lengths`: every request has at least a quarter of 4096 cached tokens, and some request has exactly 4096. `request_order`: each slot serves a different request. `expert_ids`: among the rows of one device (aligned blocks of 128 tokens) no expert is named by more than 16 rows, a bound that some block reaches.
All inputs are finite; a program needn't handle non-finite values.
Results may differ from the reference program's by a relative error of at most 0.015.
Values may be sent and summed in bfloat16 or wider, within the bound.
No kernel may reach another device: no remote copies, remote signals or barrier semaphores. Data moves between devices by JAX's collectives and lax.ppermute only.
A program may use at most 192 MiB of HBM per device.

```python
import math
import jax
import jax.numpy as jnp
import numpy as np
from jax import lax

D = 2048
HEADS = 16
HEAD = 128
EXPERTS = 64
FF = 1408
TOP = 6
CACHE = 4096
WINDOW = 4096
SINKS = 4
TOK_DEV = 128
NEW = 1024
REQUESTS = 4
TOKENS = 4096
HALF = 704
CAP = 16
N_ROW = 4
N_COL = 8


def draw_cache_keys(key, part):
    base_key = jax.random.fold_in(key, 11)
    return jax.random.normal(base_key, (REQUESTS, CACHE, HEADS * HEAD), jnp.float32).astype(jnp.bfloat16)


def draw_cached_lengths(key, part):
    lengths = jax.random.randint(jax.random.fold_in(key, 21), (REQUESTS,), CACHE // 4, CACHE + 1)
    chosen = jax.random.randint(jax.random.fold_in(key, 22), (), 0, REQUESTS)
    return jnp.where(jnp.arange(REQUESTS) == chosen, CACHE, lengths).astype(jnp.int32)


def level_of(key, dims, shards, smallest, largest):
    loudness = 1.0
    for axis_at, shards_of in shards:
        steps = jax.random.uniform(jax.random.fold_in(jax.random.fold_in(key, 6), axis_at), (shards_of,), jnp.float32, smallest / len(shards), largest / len(shards))
        loudness = loudness * jnp.repeat(jnp.exp(steps), dims[axis_at] // shards_of).reshape((-1,) + (1,) * (len(dims) - 1 - axis_at))
    return loudness


def assign_block(rng, own, number, rows, count, top, limit, skew):
    order = jax.random.permutation(rng, count)
    packed, common = portions_of(count, rows * top, limit, skew, True), portions_of(count, rows * top, limit, skew, False)
    places = jnp.arange(count)

    def named(sizes, offset_by):
        used = int((sizes > 0).sum())
        fixed = max(1, used // 4)
        passed = fixed + (places - fixed + offset_by * (used - fixed)) % max(1, count - fixed)
        return jnp.zeros((count,), jnp.int32).at[order[jnp.where(places < fixed, places, passed)]].set(jnp.asarray(sizes, jnp.int32))

    sizes = jnp.where(number % 4 == 0, named(packed, number // 4), named(common, number - number // 4 - 1))
    mixed = jax.random.permutation(jax.random.fold_in(own, 3), count)
    donor, taker = mixed[0:count // 2 * 2:2], mixed[1:count // 2 * 2:2]
    slack = jnp.minimum(sizes[donor] - 1, limit - sizes[taker]) // 2
    slack = jnp.where((donor == order[0]) | (taker == order[0]) | (sizes[taker] == 0), 0, jnp.maximum(slack, 0))
    passed = jax.random.randint(jax.random.fold_in(own, 4), (count // 2,), 0, 1 << 20) % (slack + 1)
    sizes = sizes.at[donor].add(-passed).at[taker].add(passed)
    members = jnp.searchsorted(jnp.cumsum(sizes), jnp.arange(rows * top), side="right").astype(jnp.int32)
    grid = members.reshape(top, rows).T
    grid = grid[jax.random.permutation(jax.random.fold_in(own, 1), rows)]
    offset_by = jax.random.randint(jax.random.fold_in(own, 2), (rows, 1), 0, top)
    return jnp.take_along_axis(grid, (jnp.arange(top)[None, :] + offset_by) % top, axis=1)


def portions_of(number_of, total, reach, slope, full):
    portions = [(1 << 20) // math.isqrt(standing ** slope) + 1 for standing in range(1, number_of + 1)]
    largest = reach if full else min(reach, max(-(-total // number_of), total * portions[0] // sum(portions)))
    least = 1 if total - largest >= number_of - 1 else 0
    counts, spare = [largest] + [least] * (number_of - 1), total - largest - least * (number_of - 1)
    while spare > 0:
        movable = [i for i in range(1, number_of) if counts[i] < largest] or [i for i in range(1, number_of) if counts[i] < reach]
        pool, left = sum([portions[i] for i in movable]), spare
        for i in movable:
            more = min(reach - counts[i], max(1, left * portions[i] // pool), spare)
            counts[i] = counts[i] + more
            spare = spare - more
    return np.array(counts)


def normal_values(rng, dims, deviation, reach, pieces=(), kind=jnp.bfloat16):
    result = deviation * jax.random.normal(rng, dims, jnp.float32)
    if pieces:
        result = result * level_of(rng, dims, pieces, -0.22, 0.18)
    return jnp.clip(result, -reach, reach).astype(kind)


def setup_inputs(seed: int = 0) -> dict:
    key_list = jax.random.split(jax.random.key(seed), 14)
    hidden = normal_values(key_list[0], (TOKENS, D), 1.0, 6.0, ((0, 32),))
    cached_lengths = draw_cached_lengths(jax.random.fold_in(key_list[13], 71), 0)
    request_order = jax.random.permutation(key_list[2], REQUESTS).astype(jnp.int32)
    cache_keys = draw_cache_keys(jax.random.fold_in(key_list[13], 71), 0)
    cache_values = normal_values(key_list[4], (REQUESTS, CACHE, HEADS * HEAD), 1.0, 6.0, ((0, 4), (2, 8)))
    attn_gain = jnp.clip(1.0 + 0.1 * jax.random.normal(key_list[5], (D,), jnp.float32), 0.5, 1.5).astype(jnp.bfloat16)
    w_qkv = normal_values(key_list[6], (D, HEADS, 3 * HEAD), D ** -0.5, 0.125, ((1, 8),))
    w_out = normal_values(key_list[7], (HEADS * HEAD, D), (HEADS * HEAD) ** -0.5, 0.125, ((0, 8),))
    moe_gain = jnp.clip(1.0 + 0.1 * jax.random.normal(key_list[8], (D,), jnp.float32), 0.5, 1.5).astype(jnp.bfloat16)
    expert_ids_keys = jax.random.split(jax.random.fold_in(key_list[9], 1), TOKENS // TOK_DEV)
    expert_ids_turns = jax.random.permutation(jax.random.fold_in(key_list[9], 3), TOKENS // TOK_DEV)
    expert_ids = jax.vmap(lambda own, number: assign_block(jax.random.fold_in(key_list[9], 2), own, number, TOK_DEV, EXPERTS, TOP, CAP, 1))(expert_ids_keys, expert_ids_turns).reshape((TOKENS, TOP))
    gate_weights = jnp.clip(0.049804688 + 0.3486328 * jax.random.uniform(key_list[10], (TOKENS, TOP), jnp.float32) ** level_of(key_list[10], (TOKENS, TOP), ((0, 32),), -0.2, 0.2), 0.049804688, 0.3984375).astype(jnp.bfloat16)
    w_in = normal_values(key_list[11], (2 * EXPERTS, D, FF), D ** -0.5, 0.125, ((0, 32),))
    w_down = normal_values(key_list[12], (2 * EXPERTS, HALF, D), FF ** -0.5, 0.15625, ((0, 32),))
    return dict(hidden=hidden, cached_lengths=cached_lengths, request_order=request_order, cache_keys=cache_keys, cache_values=cache_values, attn_gain=attn_gain, w_qkv=w_qkv, w_out=w_out, moe_gain=moe_gain, expert_ids=expert_ids, gate_weights=gate_weights, w_in=w_in, w_down=w_down)


EPS = 1e-06
THETA = 10000.0

def rms_scale(matrix, scaling):
    values = matrix.astype(jnp.float32)
    factor = lax.rsqrt(lax.optimization_barrier(jnp.mean(values * values, axis=-1, keepdims=True)) + EPS)
    return values * factor * scaling.astype(jnp.float32)

def rotate(vectors, positions):
    half_width = vectors.shape[-1] // 2
    frequency = THETA ** (-2.0 * jnp.arange(half_width, dtype=jnp.float32) / vectors.shape[-1])
    angles = positions.astype(jnp.float32)[..., None] * frequency
    cosine = jnp.cos(angles)[..., None, :]
    sine_part = jnp.sin(angles)[..., None, :]
    leading = vectors[..., :half_width]
    trailing = vectors[..., half_width:]
    return jnp.concatenate([leading * cosine - trailing * sine_part, trailing * cosine + leading * sine_part], axis=-1)

def attend(queries, key_rows, value_rows, key_places, key_valid, query_places):
    scores = jnp.einsum('nhe,mhe->hnm', queries.astype(jnp.float32), key_rows.astype(jnp.float32)) * queries.shape[-1] ** (-0.5)
    distance = query_places[:, None] - key_places[None, :]
    allowed = key_valid[None, :] & (distance >= 0) & ((distance < WINDOW) | (key_places[None, :] < SINKS))
    scores = jnp.where(allowed[None], scores, -1e+30)
    highest = lax.optimization_barrier(jnp.max(scores, axis=-1, keepdims=True))
    weights = jnp.exp(scores - highest)
    shares = (weights / lax.optimization_barrier(jnp.sum(weights, axis=-1, keepdims=True))).astype(jnp.bfloat16)
    return jnp.einsum('hnm,mhe->nhe', shares.astype(jnp.float32), value_rows.astype(jnp.float32)).astype(jnp.bfloat16)

def request_attention(operands):
    queries, fresh_keys, fresh_values, old_keys, old_values, length = operands
    places = jnp.arange(CACHE, dtype=jnp.int32)
    query_places = length + jnp.arange(NEW, dtype=jnp.int32)
    key_places = jnp.concatenate([places, query_places])
    key_valid = jnp.concatenate([places < length, jnp.ones((NEW,), jnp.bool_)])
    key_rows = jnp.concatenate([old_keys.reshape(CACHE, HEADS, HEAD), fresh_keys], axis=0)
    value_rows = jnp.concatenate([old_values.reshape(CACHE, HEADS, HEAD), fresh_values], axis=0)

    def one_head(head_operands):
        head_queries, head_keys, head_values = head_operands
        return attend(head_queries[:, None], head_keys[:, None], head_values[:, None], key_places, key_valid, query_places)[:, 0]
    per_head = lax.map(one_head, (queries.transpose(1, 0, 2), key_rows.transpose(1, 0, 2), value_rows.transpose(1, 0, 2)))
    return per_head.transpose(1, 0, 2)

def reference(hidden, cached_lengths, request_order, cache_keys, cache_values, attn_gain, w_qkv, w_out, moe_gain, expert_ids, gate_weights, w_in, w_down):
    normed = rms_scale(hidden, attn_gain).astype(jnp.bfloat16)
    projected = jnp.dot(normed, w_qkv.reshape(D, HEADS * 3 * HEAD), preferred_element_type=jnp.float32)
    projected = projected.reshape(REQUESTS, NEW, HEADS, 3, HEAD)
    lengths = cached_lengths[request_order]
    positions = lengths[:, None] + jnp.arange(NEW, dtype=jnp.int32)[None, :]
    queries = rotate(projected[..., 0, :], positions).astype(jnp.bfloat16)
    new_keys = rotate(projected[..., 1, :], positions).astype(jnp.bfloat16)
    new_values = projected[..., 2, :].astype(jnp.bfloat16)
    context = lax.map(request_attention, (queries, new_keys, new_values, cache_keys, cache_values, lengths))
    context = context.reshape(TOKENS, HEADS * HEAD)
    group_width = HEADS * HEAD // N_COL

    def add_group(running, group_index):
        offset = (group_index * group_width).astype(jnp.int32)
        partial_value = jnp.dot(lax.dynamic_slice_in_dim(context, offset, group_width, 1), lax.dynamic_slice_in_dim(w_out, offset, group_width, 0), preferred_element_type=jnp.float32)
        rounded = lax.optimization_barrier(partial_value.astype(jnp.bfloat16))
        return (running + rounded.astype(jnp.float32), None)
    attention, unused = lax.scan(add_group, jnp.zeros((TOKENS, D), jnp.float32), jnp.arange(N_COL, dtype=jnp.int32))
    residual = hidden.astype(jnp.float32) + attention
    moe_in = rms_scale(residual, moe_gain).astype(jnp.bfloat16)
    flat_ids = expert_ids.reshape(-1)
    onehot = (flat_ids[:, None] == jnp.arange(EXPERTS, dtype=jnp.int32)[None, :]).astype(jnp.int32)
    slot_rank = lax.optimization_barrier(jnp.sum((jnp.cumsum(onehot, axis=0) - onehot) * onehot, axis=1))
    capacity = CAP * N_ROW * N_COL
    owners = jnp.arange(TOKENS * TOP, dtype=jnp.int32) // TOP
    slot_table = jnp.full((EXPERTS, capacity), TOKENS, jnp.int32).at[flat_ids, slot_rank].set(owners)
    gate_table = jnp.zeros((EXPERTS, capacity), jnp.float32).at[flat_ids, slot_rank].set(gate_weights.reshape(-1).astype(jnp.float32))
    padded = jnp.concatenate([moe_in, jnp.zeros((1, D), jnp.bfloat16)], axis=0)
    inner = w_in.reshape(EXPERTS, 2, D, FF)
    outer = w_down.reshape(EXPERTS, 2, HALF, D)

    def one_expert(accumulated, operands):
        indices, gates, expert_in, expert_out = operands
        features = padded[indices]
        combined = jnp.zeros((capacity, D), jnp.float32)
        for half_index in range(2):
            both_parts = jnp.dot(features, expert_in[half_index], preferred_element_type=jnp.float32)
            activated = (jax.nn.silu(both_parts[:, :HALF]) * both_parts[:, HALF:]).astype(jnp.bfloat16)
            combined = combined + jnp.dot(activated, expert_out[half_index], preferred_element_type=jnp.float32)
        rounded = lax.optimization_barrier(combined.astype(jnp.bfloat16))
        return (accumulated.at[indices].add(gates[:, None] * rounded.astype(jnp.float32)), None)
    expert_sum, unused = lax.scan(one_expert, jnp.zeros((TOKENS + 1, D), jnp.float32), (slot_table, gate_table, inner, outer))
    new_hidden = (residual + expert_sum[:TOKENS]).astype(jnp.bfloat16)
    return (new_hidden, new_keys.reshape(TOKENS, HEADS * HEAD), new_values.reshape(TOKENS, HEADS * HEAD))
```

```python
import functools

import jax
import jax.numpy as jnp
from jax import lax
from jax.experimental import pallas as pl
from jax.experimental.pallas import tpu as pltpu
from jax.sharding import PartitionSpec as P

EXPERTS = 64
WINDOW = 4096
SINKS = 4
CAP = 16
HEAD = 128

EPS = 1e-06
THETA = 10000.0
LOG2E = 1.4426950408889634
NEG = -1e30
MIB = 1 << 20


def rms_scale(matrix, scaling):
    values = matrix.astype(jnp.float32)
    factor = lax.rsqrt(jnp.mean(values * values, axis=-1, keepdims=True) + EPS)
    return values * factor * scaling.astype(jnp.float32)


def qkv_kernel(heads, x_ref, w_ref, cos_ref, sin_ref, q_ref, k_ref, v_ref):
    projected = jnp.dot(x_ref[...], w_ref[...], preferred_element_type=jnp.float32)
    cosine = cos_ref[...]
    sine = sin_ref[...]
    for h in range(heads):
        base = h * 3 * HEAD
        out = slice(h * HEAD, (h + 1) * HEAD)
        q = projected[:, base : base + HEAD]
        k = projected[:, base + HEAD : base + 2 * HEAD]
        q = q * cosine + pltpu.roll(q, HEAD // 2, 1) * sine
        k = k * cosine + pltpu.roll(k, HEAD // 2, 1) * sine
        q_ref[:, out] = (q * (LOG2E * HEAD**-0.5)).astype(jnp.bfloat16)
        k_ref[:, out] = k.astype(jnp.bfloat16)
        v_ref[:, out] = projected[:, base + 2 * HEAD : base + 3 * HEAD].astype(jnp.bfloat16)


def qkv_call(x, w, cosine, sine, heads, block=256):
    rows, width = x.shape
    out = jax.ShapeDtypeStruct((rows, heads * HEAD), jnp.bfloat16)
    out_spec = pl.BlockSpec((block, heads * HEAD), lambda i: (i, 0))
    return pl.pallas_call(
        functools.partial(qkv_kernel, heads),
        grid=(rows // block,),
        in_specs=[
            pl.BlockSpec((block, width), lambda i: (i, 0)),
            pl.BlockSpec(w.shape, lambda i: (0, 0)),
            pl.BlockSpec((block, HEAD), lambda i: (i, 0)),
            pl.BlockSpec((block, HEAD), lambda i: (i, 0)),
        ],
        out_specs=[out_spec] * 3,
        out_shape=[out] * 3,
        compiler_params=pltpu.CompilerParams(vmem_limit_bytes=32 * MIB),
        cost_estimate=pl.CostEstimate(
            flops=2 * rows * width * w.shape[1],
            bytes_accessed=2 * (rows * width + w.size + 3 * rows * heads * HEAD),
            transcendentals=0,
        ),
        name="qkv",
    )(x, w, cosine, sine)


def attention_kernel(heads, bq, bk, len_ref, q_ref, kc_ref, vc_ref, kn_ref, vn_ref, o_ref):
    q_start = pl.program_id(0) * bq
    length = len_ref[0]
    first = length + q_start
    last = first + bq - 1
    blocks = (length + bk - 1) // bk
    lowest = jnp.maximum(first - WINDOW + 1, 0) // bk
    inside = jnp.minimum((jnp.maximum(last - WINDOW + 1, 0) + bk - 1) // bk, blocks)
    whole = jnp.maximum(inside, length // bk)

    def update(state, keys, values, allowed):
        new_state = []
        for h in range(heads):
            m, l, acc = state[h]
            cols = slice(h * HEAD, (h + 1) * HEAD)
            s = lax.dot_general(
                q_ref[:, cols],
                keys[h],
                (((1,), (1,)), ((), ())),
                preferred_element_type=jnp.float32,
            )
            if allowed is not None:
                s = jnp.where(allowed, s, NEG)
            m_new = jnp.maximum(m, jnp.max(s, axis=1, keepdims=True))
            alpha = jnp.exp2(m - m_new)
            p = jnp.exp2(s - m_new)
            l = l * alpha + jnp.sum(p, axis=1, keepdims=True)
            acc = acc * alpha + jnp.dot(
                p.astype(jnp.bfloat16), values[h], preferred_element_type=jnp.float32
            )
            new_state.append((m_new, l, acc))
        return tuple(new_state)

    def cached(start, size):
        keys = [kc_ref[0, pl.ds(start, size), h * HEAD : (h + 1) * HEAD] for h in range(heads)]
        values = [vc_ref[0, pl.ds(start, size), h * HEAD : (h + 1) * HEAD] for h in range(heads)]
        return keys, values

    def fresh(start, size):
        keys = [kn_ref[pl.ds(start, size), h * HEAD : (h + 1) * HEAD] for h in range(heads)]
        values = [vn_ref[pl.ds(start, size), h * HEAD : (h + 1) * HEAD] for h in range(heads)]
        return keys, values

    def sink_step(j, state):
        places = lax.broadcasted_iota(jnp.int32, (bq, HEAD), 1)
        rows = lax.broadcasted_iota(jnp.int32, (bq, HEAD), 0)
        allowed = (places < SINKS) & (places < lowest * bk) & (first + rows - places >= WINDOW)
        return update(state, *cached(0, HEAD), allowed)

    def masked_step(j, state):
        start = pl.multiple_of(j * bk, bk)
        places = start + lax.broadcasted_iota(jnp.int32, (bq, bk), 1)
        rows = lax.broadcasted_iota(jnp.int32, (bq, bk), 0)
        allowed = (places < length) & ((first + rows - places < WINDOW) | (places < SINKS))
        return update(state, *cached(start, bk), allowed)

    def plain_step(j, state):
        return update(state, *cached(pl.multiple_of(j * bk, bk), bk), None)

    def fresh_step(j, state):
        return update(state, *fresh(pl.multiple_of(j * bq, bq), bq), None)

    state = tuple(
        (
            jnp.full((bq, 1), NEG, jnp.float32),
            jnp.zeros((bq, 1), jnp.float32),
            jnp.zeros((bq, HEAD), jnp.float32),
        )
        for h in range(heads)
    )
    state = lax.fori_loop(0, jnp.minimum(lowest, 1), sink_step, state)
    state = lax.fori_loop(lowest, inside, masked_step, state)
    state = lax.fori_loop(inside, whole, plain_step, state)
    state = lax.fori_loop(whole, blocks, masked_step, state)
    state = lax.fori_loop(0, pl.program_id(0), fresh_step, state)
    rows = lax.broadcasted_iota(jnp.int32, (bq, bq), 0)
    places = lax.broadcasted_iota(jnp.int32, (bq, bq), 1)
    state = update(state, *fresh(pl.multiple_of(q_start, bq), bq), places <= rows)
    for h in range(heads):
        m, l, acc = state[h]
        o_ref[:, h * HEAD : (h + 1) * HEAD] = (acc / l).astype(o_ref.dtype)


def attention_call(length, q, cache_keys, cache_values, new_keys, new_values, bq=256, bk=512):
    rows, width = q.shape
    heads = width // HEAD
    cache_rows = cache_keys.shape[1]
    bk = min(bk, cache_rows)
    fixed = lambda shape: pl.BlockSpec(shape, lambda i, n: (0,) * len(shape))
    return pl.pallas_call(
        functools.partial(attention_kernel, heads, bq, bk),
        grid_spec=pltpu.PrefetchScalarGridSpec(
            num_scalar_prefetch=1,
            grid=(rows // bq,),
            in_specs=[
                pl.BlockSpec((bq, width), lambda i, n: (i, 0)),
                fixed(cache_keys.shape),
                fixed(cache_values.shape),
                fixed(new_keys.shape),
                fixed(new_values.shape),
            ],
            out_specs=pl.BlockSpec((bq, width), lambda i, n: (i, 0)),
        ),
        out_shape=jax.ShapeDtypeStruct((rows, width), jnp.bfloat16),
        compiler_params=pltpu.CompilerParams(vmem_limit_bytes=40 * MIB),
        cost_estimate=pl.CostEstimate(
            flops=4 * rows * width * (cache_rows + rows),
            bytes_accessed=4 * (cache_rows + 2 * rows) * width,
            transcendentals=rows * heads * (cache_rows + rows),
        ),
        name="attention",
    )(length, q, cache_keys, cache_values, new_keys, new_values)


def project_kernel(x_ref, w_ref, hidden_ref, gain_ref, resid_ref, normed_ref):
    g = pl.program_id(0)
    share = jnp.dot(x_ref[0], w_ref[0], preferred_element_type=jnp.float32)
    share = share.astype(jnp.bfloat16).astype(jnp.float32)

    @pl.when(g == 0)
    def _():
        resid_ref[...] = share

    @pl.when(g > 0)
    def _():
        resid_ref[...] += share

    @pl.when(g == pl.num_programs(0) - 1)
    def _():
        resid = resid_ref[...] + hidden_ref[...].astype(jnp.float32)
        resid_ref[...] = resid
        normed_ref[...] = rms_scale(resid, gain_ref[...]).astype(jnp.bfloat16)


def project_call(x, w, hidden, gain):
    groups, rows, width = x.shape
    model = w.shape[2]
    fixed = pl.BlockSpec((rows, model), lambda g: (0, 0))
    return pl.pallas_call(
        project_kernel,
        grid=(groups,),
        in_specs=[
            pl.BlockSpec((1, rows, width), lambda g: (g, 0, 0)),
            pl.BlockSpec((1, width, model), lambda g: (g, 0, 0)),
            fixed,
            pl.BlockSpec((1, model), lambda g: (0, 0)),
        ],
        out_specs=[fixed, fixed],
        out_shape=[
            jax.ShapeDtypeStruct((rows, model), jnp.float32),
            jax.ShapeDtypeStruct((rows, model), jnp.bfloat16),
        ],
        compiler_params=pltpu.CompilerParams(vmem_limit_bytes=24 * MIB),
        cost_estimate=pl.CostEstimate(
            flops=2 * rows * model * groups * width,
            bytes_accessed=2 * (w.size + x.size) + 8 * rows * model,
            transcendentals=0,
        ),
        name="project",
    )(x, w, hidden, gain.reshape(1, model))


def expert_kernel(half, x_ref, win_ref, wdown_ref, o_ref, acc_ref):
    h = pl.program_id(1)
    senders, unused, slots, width = x_ref.shape
    x = x_ref[...].reshape(senders * slots, width)
    both = jnp.dot(x, win_ref[0], preferred_element_type=jnp.float32)
    a = both[:, :half]
    b = both[:, half:]
    act = (a / (1.0 + jnp.exp(-a)) * b).astype(jnp.bfloat16)
    part = jnp.dot(act, wdown_ref[0], preferred_element_type=jnp.float32)

    @pl.when(h == 0)
    def _():
        acc_ref[...] = part

    @pl.when(h > 0)
    def _():
        acc_ref[...] += part

    @pl.when(h == pl.num_programs(1) - 1)
    def _():
        o_ref[...] = acc_ref[...].astype(jnp.bfloat16).reshape(o_ref.shape)


def expert_call(x, w_in, w_down, halves):
    senders, experts, slots, width = x.shape
    units, model = w_down.shape[1:]
    rows = senders * slots
    block = pl.BlockSpec((senders, 1, slots, width), lambda e, h: (0, e, 0, 0))
    return pl.pallas_call(
        functools.partial(expert_kernel, units),
        grid=(experts, halves),
        in_specs=[
            block,
            pl.BlockSpec((1, width, 2 * units), lambda e, h: (e * halves + h, 0, 0)),
            pl.BlockSpec((1, units, model), lambda e, h: (e * halves + h, 0, 0)),
        ],
        out_specs=block,
        out_shape=jax.ShapeDtypeStruct(x.shape, jnp.bfloat16),
        scratch_shapes=[pltpu.VMEM((rows, model), jnp.float32)],
        compiler_params=pltpu.CompilerParams(vmem_limit_bytes=56 * MIB),
        cost_estimate=pl.CostEstimate(
            flops=6 * rows * experts * halves * width * units,
            bytes_accessed=2 * (w_in.size + w_down.size + 2 * x.size),
            transcendentals=rows * experts * halves * units,
        ),
        name="experts",
    )(x, w_in, w_down)


def body(
    hidden,
    cached_lengths,
    request_order,
    cache_keys,
    cache_values,
    attn_gain,
    w_qkv,
    w_out,
    moe_gain,
    expert_ids,
    gate_weights,
    w_in,
    w_down,
):
    tok_rows, model_width = hidden.shape
    heads_here = w_qkv.shape[1]
    row_count = lax.axis_size("row")
    col_count = lax.axis_size("col")
    device_count = row_count * col_count
    new_rows = tok_rows * col_count

    normed = rms_scale(hidden, attn_gain).astype(jnp.bfloat16)
    gathered = lax.all_gather(normed, "col", axis=0, tiled=True)
    w_out_all = lax.all_gather(w_out, "col", axis=0)

    row_index = lax.axis_index("row")
    places = jnp.arange(request_order.shape[0], dtype=jnp.int32)
    request = jnp.sum(jnp.where(places == row_index, request_order, 0))
    length = jnp.sum(jnp.where(places == request, cached_lengths, 0))
    query_pos = length + jnp.arange(new_rows, dtype=jnp.int32)
    frequency = THETA ** (-2.0 * jnp.arange(HEAD // 2, dtype=jnp.float32) / HEAD)
    angles = query_pos.astype(jnp.float32)[:, None] * frequency
    cosine, sine = jnp.cos(angles), jnp.sin(angles)
    cosine = jnp.concatenate([cosine, cosine], axis=1)
    sine = jnp.concatenate([-sine, sine], axis=1)

    queries, new_keys, new_values = qkv_call(
        gathered, w_qkv.reshape(model_width, -1), cosine, sine, heads_here
    )
    context = attention_call(
        length.reshape(1), queries, cache_keys, cache_values, new_keys, new_values
    )
    shares = lax.all_to_all(
        context.reshape(col_count, tok_rows, heads_here * HEAD), "col", 0, 0, tiled=True
    )
    residual, moe_in = project_call(shares, w_out_all, hidden, moe_gain)

    chosen = expert_ids[:, :, None] == jnp.arange(EXPERTS, dtype=jnp.int32)
    named = jnp.any(chosen, axis=1)
    gates = jnp.sum(jnp.where(chosen, gate_weights.astype(jnp.float32)[:, :, None], 0.0), axis=1)
    earlier = jnp.arange(tok_rows)[:, None] > jnp.arange(tok_rows)[None, :]
    rank = jnp.dot(
        earlier.astype(jnp.bfloat16),
        named.astype(jnp.bfloat16),
        preferred_element_type=jnp.float32,
    ).astype(jnp.int32)
    rank = jnp.where(named, rank, -1)
    place = (rank[:, :, None] == jnp.arange(CAP, dtype=jnp.int32)).reshape(tok_rows, EXPERTS * CAP)
    place_gates = jnp.where(place, jnp.repeat(gates, CAP, axis=1), 0.0).astype(jnp.bfloat16)

    per_device = w_in.shape[0]
    halves = 2 if per_device % 2 == 0 else 1
    copies = 2 // halves
    routed = lax.dot_general(
        place.astype(jnp.bfloat16),
        moe_in,
        (((0,), (0,)), ((), ())),
        preferred_element_type=jnp.float32,
    ).astype(jnp.bfloat16)
    routed = routed.reshape(EXPERTS, 1, CAP, model_width)
    routed = jnp.broadcast_to(routed, (EXPERTS, copies, CAP, model_width))
    routed = routed.reshape(device_count, per_device // halves, CAP, model_width)
    received = lax.all_to_all(routed, ("row", "col"), split_axis=0, concat_axis=0, tiled=True)
    parts = expert_call(received, w_in, w_down, halves)
    returned = lax.all_to_all(parts, ("row", "col"), split_axis=0, concat_axis=0, tiled=True)
    if copies > 1:
        returned = returned.reshape(EXPERTS, copies, CAP, model_width).astype(jnp.float32)
        returned = jnp.sum(returned, axis=1).astype(jnp.bfloat16)
    returned = returned.reshape(EXPERTS * CAP, model_width)
    expert_sum = jnp.dot(place_gates, returned, preferred_element_type=jnp.float32)
    new_hidden = (residual + expert_sum).astype(jnp.bfloat16)
    return (new_hidden, new_keys, new_values)


def solution(mesh):
    in_specs = (
        P(("row", "col"), None),
        P(),
        P(),
        P("row", None, "col"),
        P("row", None, "col"),
        P(),
        P(None, "col", None),
        P("col", None),
        P(),
        P(("row", "col"), None),
        P(("row", "col"), None),
        P(("row", "col"), None, None),
        P(("row", "col"), None, None),
    )
    out_specs = (P(("row", "col"), None), P("row", "col"), P("row", "col"))
    return jax.shard_map(body, mesh=mesh, in_specs=in_specs, out_specs=out_specs, check_vma=False)
```

```python
import functools

import jax
import jax.numpy as jnp
from jax import lax
from jax.experimental import pallas as pl
from jax.experimental.pallas import tpu as pltpu
from jax.sharding import PartitionSpec as P

EXPERTS = 64
WINDOW = 4096
SINKS = 4
CAP = 16
HEAD = 128

EPS = 1e-06
THETA = 10000.0
LOG2E = 1.4426950408889634
NEG = -1e30
MIB = 1 << 20


def rms_scale(matrix, scaling):
    values = matrix.astype(jnp.float32)
    factor = lax.rsqrt(jnp.mean(values * values, axis=-1, keepdims=True) + EPS)
    return values * factor * scaling.astype(jnp.float32)


def qkv_kernel(heads, order_ref, x_ref, w_ref, cos_ref, sin_ref, *refs):
    q_ref, k_ref, v_ref = refs[-3:]
    projected = jnp.dot(x_ref[...], w_ref[...], preferred_element_type=jnp.float32)
    cosine = cos_ref[...]
    sine = sin_ref[...]
    for h in range(heads):
        base = h * 3 * HEAD
        out = slice(h * HEAD, (h + 1) * HEAD)
        q = projected[:, base : base + HEAD]
        k = projected[:, base + HEAD : base + 2 * HEAD]
        q = q * cosine + pltpu.roll(q, HEAD // 2, 1) * sine
        k = k * cosine + pltpu.roll(k, HEAD // 2, 1) * sine
        q_ref[:, out] = (q * (LOG2E * HEAD**-0.5)).astype(jnp.bfloat16)
        k_ref[:, out] = k.astype(jnp.bfloat16)
        v_ref[:, out] = projected[:, base + 2 * HEAD : base + 3 * HEAD].astype(jnp.bfloat16)


def qkv_call(order, x, w, cosine, sine, heads, before=()):
    rows, width = x.shape
    total = cosine.shape[0]
    block = rows // order.shape[0]
    out = jax.ShapeDtypeStruct((total, heads * HEAD), jnp.bfloat16)
    placed = lambda i, n: (n[i], 0)
    out_spec = pl.BlockSpec((block, heads * HEAD), placed)
    return pl.pallas_call(
        functools.partial(qkv_kernel, heads),
        grid_spec=pltpu.PrefetchScalarGridSpec(
            num_scalar_prefetch=1,
            grid=(rows // block,),
            in_specs=[
                pl.BlockSpec((block, width), lambda i, n: (i, 0)),
                pl.BlockSpec(w.shape, lambda i, n: (0, 0)),
                pl.BlockSpec((block, HEAD), placed),
                pl.BlockSpec((block, HEAD), placed),
            ]
            + [pl.BlockSpec(memory_space=pl.ANY)] * len(before),
            out_specs=[out_spec] * 3,
        ),
        out_shape=[out] * 3,
        input_output_aliases={5 + i: i for i in range(len(before))},
        compiler_params=pltpu.CompilerParams(vmem_limit_bytes=24 * MIB),
        cost_estimate=pl.CostEstimate(
            flops=2 * rows * width * w.shape[1],
            bytes_accessed=2 * (rows * width + w.size + 3 * rows * heads * HEAD),
            transcendentals=0,
        ),
        name="qkv",
    )(order, x, w, cosine, sine, *before)


def attention_kernel(heads, bq, bk, len_ref, q_ref, kc_ref, vc_ref, kn_ref, vn_ref, o_ref):
    q_start = pl.program_id(0) * bq
    length = len_ref[0]
    first = length + q_start
    last = first + bq - 1
    blocks = (length + bk - 1) // bk
    lowest = jnp.maximum(first - WINDOW + 1, 0) // bk
    inside = jnp.minimum((jnp.maximum(last - WINDOW + 1, 0) + bk - 1) // bk, blocks)
    whole = jnp.maximum(inside, length // bk)

    def update(state, keys, values, allowed):
        new_state = []
        for h in range(heads):
            m, l, acc = state[h]
            cols = slice(h * HEAD, (h + 1) * HEAD)
            s = lax.dot_general(
                q_ref[:, cols],
                keys[h],
                (((1,), (1,)), ((), ())),
                preferred_element_type=jnp.float32,
            )
            if allowed is not None:
                s = jnp.where(allowed, s, NEG)
            m_new = jnp.maximum(m, jnp.max(s, axis=1, keepdims=True))
            alpha = jnp.exp2(m - m_new)
            p = jnp.exp2(s - m_new)
            l = l * alpha + jnp.sum(p, axis=1, keepdims=True)
            acc = acc * alpha + jnp.dot(
                p.astype(jnp.bfloat16), values[h], preferred_element_type=jnp.float32
            )
            new_state.append((m_new, l, acc))
        return tuple(new_state)

    def cached(start, size):
        keys = [kc_ref[0, pl.ds(start, size), h * HEAD : (h + 1) * HEAD] for h in range(heads)]
        values = [vc_ref[0, pl.ds(start, size), h * HEAD : (h + 1) * HEAD] for h in range(heads)]
        return keys, values

    def fresh(start, size):
        keys = [kn_ref[pl.ds(start, size), h * HEAD : (h + 1) * HEAD] for h in range(heads)]
        values = [vn_ref[pl.ds(start, size), h * HEAD : (h + 1) * HEAD] for h in range(heads)]
        return keys, values

    def sink_step(j, state):
        places = lax.broadcasted_iota(jnp.int32, (bq, HEAD), 1)
        rows = lax.broadcasted_iota(jnp.int32, (bq, HEAD), 0)
        allowed = (places < SINKS) & (places < lowest * bk) & (first + rows - places >= WINDOW)
        return update(state, *cached(0, HEAD), allowed)

    def masked_step(j, state):
        start = pl.multiple_of(j * bk, bk)
        places = start + lax.broadcasted_iota(jnp.int32, (bq, bk), 1)
        rows = lax.broadcasted_iota(jnp.int32, (bq, bk), 0)
        allowed = (places < length) & ((first + rows - places < WINDOW) | (places < SINKS))
        return update(state, *cached(start, bk), allowed)

    def plain_step(j, state):
        return update(state, *cached(pl.multiple_of(j * bk, bk), bk), None)

    def fresh_step(j, state):
        return update(state, *fresh(pl.multiple_of(j * bq, bq), bq), None)

    state = tuple(
        (
            jnp.full((bq, 1), NEG, jnp.float32),
            jnp.zeros((bq, 1), jnp.float32),
            jnp.zeros((bq, HEAD), jnp.float32),
        )
        for h in range(heads)
    )
    state = lax.fori_loop(0, jnp.minimum(lowest, 1), sink_step, state)
    state = lax.fori_loop(lowest, inside, masked_step, state)
    state = lax.fori_loop(inside, whole, plain_step, state)
    state = lax.fori_loop(whole, blocks, masked_step, state)
    state = lax.fori_loop(0, pl.program_id(0), fresh_step, state)
    rows = lax.broadcasted_iota(jnp.int32, (bq, bq), 0)
    places = lax.broadcasted_iota(jnp.int32, (bq, bq), 1)
    state = update(state, *fresh(pl.multiple_of(q_start, bq), bq), places <= rows)
    for h in range(heads):
        m, l, acc = state[h]
        o_ref[:, h * HEAD : (h + 1) * HEAD] = (acc / l).astype(o_ref.dtype)


def attention_call(length, q, cache_keys, cache_values, new_keys, new_values, bq=256, bk=512):
    rows, width = q.shape
    heads = width // HEAD
    cache_rows = cache_keys.shape[1]
    bk = min(bk, cache_rows)
    fixed = lambda shape: pl.BlockSpec(shape, lambda i, n: (0,) * len(shape))
    return pl.pallas_call(
        functools.partial(attention_kernel, heads, bq, bk),
        grid_spec=pltpu.PrefetchScalarGridSpec(
            num_scalar_prefetch=1,
            grid=(rows // bq,),
            in_specs=[
                pl.BlockSpec((bq, width), lambda i, n: (i, 0)),
                fixed(cache_keys.shape),
                fixed(cache_values.shape),
                fixed(new_keys.shape),
                fixed(new_values.shape),
            ],
            out_specs=pl.BlockSpec((bq, width), lambda i, n: (i, 0)),
        ),
        out_shape=jax.ShapeDtypeStruct((rows, width), jnp.bfloat16),
        compiler_params=pltpu.CompilerParams(vmem_limit_bytes=40 * MIB),
        cost_estimate=pl.CostEstimate(
            flops=4 * rows * width * (cache_rows + rows),
            bytes_accessed=4 * (cache_rows + 2 * rows) * width,
            transcendentals=rows * heads * (cache_rows + rows),
        ),
        name="attention",
    )(length, q, cache_keys, cache_values, new_keys, new_values)


def project_kernel(parts, order_ref, *refs):
    x_refs, w_refs = refs[:parts], refs[parts : 2 * parts]
    hidden_ref, gain_ref, resid_ref, normed_ref = refs[2 * parts :]
    g = pl.program_id(0)

    @pl.when(g == 0)
    def _():
        resid_ref[...] = hidden_ref[...].astype(jnp.float32)

    for x_ref, w_ref in zip(x_refs, w_refs):
        share = jnp.dot(x_ref[0], w_ref[0], preferred_element_type=jnp.float32)
        resid_ref[...] += share.astype(jnp.bfloat16).astype(jnp.float32)

    @pl.when(g == pl.num_programs(0) - 1)
    def _():
        normed_ref[...] = rms_scale(resid_ref[...], gain_ref[...]).astype(jnp.bfloat16)


def project_call(order, x, weights, hidden, gain):
    groups, rows, width = x.shape
    parts = len(weights)
    steps, unused, model = weights[0].shape
    fixed = pl.BlockSpec((rows, model), lambda g, n: (0, 0))

    def share_spec(part):
        return pl.BlockSpec((1, rows, width), lambda g, n: (n[g * parts + part], 0, 0))

    return pl.pallas_call(
        functools.partial(project_kernel, parts),
        grid_spec=pltpu.PrefetchScalarGridSpec(
            num_scalar_prefetch=1,
            grid=(steps,),
            in_specs=[share_spec(part) for part in range(parts)]
            + [pl.BlockSpec((1, width, model), lambda g, n: (g, 0, 0))] * parts
            + [fixed, pl.BlockSpec((1, model), lambda g, n: (0, 0))],
            out_specs=[fixed, fixed],
        ),
        out_shape=[
            jax.ShapeDtypeStruct((rows, model), jnp.float32),
            jax.ShapeDtypeStruct((rows, model), jnp.bfloat16),
        ],
        compiler_params=pltpu.CompilerParams(vmem_limit_bytes=24 * MIB),
        cost_estimate=pl.CostEstimate(
            flops=2 * rows * model * groups * width,
            bytes_accessed=2 * groups * (width * model + rows * width) + 8 * rows * model,
            transcendentals=0,
        ),
        name="project",
    )(order, *[x] * parts, *weights, hidden, gain.reshape(1, model))


def expert_kernel(half, counts, resident, *refs):
    x_refs = refs[: len(counts)]
    win_ref, wdown_ref = refs[len(counts) : len(counts) + 2]
    o_refs, acc_ref = refs[len(counts) + 2 : -1], refs[-1]
    h = pl.program_id(1)
    width = x_refs[0].shape[-1]
    x = [ref[...].reshape(-1, width) for ref in x_refs]
    x = x[0] if len(x) == 1 else jnp.concatenate(x, axis=0)
    at = pl.program_id(0) * pl.num_programs(1) + h if resident else 0
    both = jnp.dot(x, win_ref[at], preferred_element_type=jnp.float32)
    a = both[:, :half]
    b = both[:, half:]
    act = (a / (1.0 + jnp.exp(-a)) * b).astype(jnp.bfloat16)
    part = jnp.dot(act, wdown_ref[0], preferred_element_type=jnp.float32)

    @pl.when(h == 0)
    def _():
        acc_ref[...] = part

    @pl.when(h > 0)
    def _():
        acc_ref[...] += part

    @pl.when(h == pl.num_programs(1) - 1)
    def _():
        start = 0
        for ref in o_refs:
            size = ref.shape[0] * ref.shape[2]
            ref[...] = acc_ref[start : start + size].astype(jnp.bfloat16).reshape(ref.shape)
            start += size


def expert_call(xs, takes, outs, w_in, w_down, halves, resident=False):
    unused, unused, slots, width = xs[0].shape
    experts = w_in.shape[0] // halves
    units, model = w_down.shape[1:]
    rows = sum(takes) * slots
    block = lambda senders: pl.BlockSpec((senders, 1, slots, width), lambda e, h: (0, e, 0, 0))
    weight_specs = [
        pl.BlockSpec((1, width, 2 * units), lambda e, h: (e * halves + h, 0, 0)),
        pl.BlockSpec((1, units, model), lambda e, h: (e * halves + h, 0, 0)),
    ]
    if resident:
        weight_specs[0] = pl.BlockSpec(memory_space=pltpu.VMEM)
    return pl.pallas_call(
        functools.partial(expert_kernel, units, takes, resident),
        grid=(experts, halves),
        in_specs=[block(senders) for senders in takes] + weight_specs,
        out_specs=[block(senders) for senders in outs],
        out_shape=[
            jax.ShapeDtypeStruct((senders, experts, slots, width), jnp.bfloat16) for senders in outs
        ],
        scratch_shapes=[pltpu.VMEM((rows, model), jnp.float32)],
        compiler_params=pltpu.CompilerParams(vmem_limit_bytes=(24 if resident else 56) * MIB),
        cost_estimate=pl.CostEstimate(
            flops=6 * rows * experts * halves * width * units,
            bytes_accessed=2 * (w_in.size + w_down.size + 2 * rows * experts * width),
            transcendentals=rows * experts * halves * units,
        ),
        name="experts",
    )(*xs, w_in, w_down)


def xor_pairs(count, bits):
    return [(i, i ^ bits) for i in range(count)]


def gather_plane(block, later):
    rows = block.shape[0]
    along_x = lax.ppermute(block, "col", xor_pairs(8, 2))
    along_y = lax.ppermute(block, "col", xor_pairs(8, 4))
    along_x, along_y, later = lax.optimization_barrier((along_x, along_y, later))
    across_0 = lax.ppermute(along_x[: rows // 2], "col", xor_pairs(8, 4))
    across_1 = lax.ppermute(along_y[rows // 2 :], "col", xor_pairs(8, 2))
    mine = jnp.concatenate([block, along_x, along_y, across_0, across_1], axis=0)
    return mine, lax.ppermute(mine, "col", xor_pairs(8, 1)), later


def slot_places(ids, gates, experts):
    rows = ids.shape[-2]
    chosen = ids[..., None] == experts
    named = jnp.any(chosen, axis=-2)
    weight = jnp.sum(jnp.where(chosen, gates[..., None], 0.0), axis=-2)
    earlier = jnp.arange(rows)[:, None] > jnp.arange(rows)[None, :]
    rank = jnp.einsum(
        "ij,...je->...ie",
        earlier.astype(jnp.bfloat16),
        named.astype(jnp.bfloat16),
        preferred_element_type=jnp.float32,
    ).astype(jnp.int32)
    rank = jnp.where(named, rank, -1)
    place = rank[..., None] == jnp.arange(CAP, dtype=jnp.int32)
    gated = jnp.where(place, weight[..., None], 0.0).astype(jnp.bfloat16)
    flat = ids.shape[:-1] + (experts.shape[0] * CAP,)
    return place.reshape(flat).astype(jnp.bfloat16), gated.reshape(flat)


def route(place, rows):
    return lax.dot_general(
        place, rows, (((0,), (0,)), ((), ())), preferred_element_type=jnp.float32
    ).astype(jnp.bfloat16)


def experts_direct(moe_in, residual, expert_ids, gate_weights, w_in, w_down):
    tok_rows, model_width = moe_in.shape
    device_count = lax.axis_size("row") * lax.axis_size("col")
    place, place_gates = slot_places(
        expert_ids, gate_weights.astype(jnp.float32), jnp.arange(EXPERTS, dtype=jnp.int32)
    )
    per_device = w_in.shape[0]
    halves = 2 if per_device % 2 == 0 else 1
    copies = 2 // halves
    routed = route(place, moe_in).reshape(EXPERTS, 1, CAP, model_width)
    routed = jnp.broadcast_to(routed, (EXPERTS, copies, CAP, model_width))
    routed = routed.reshape(device_count, per_device // halves, CAP, model_width)
    received = lax.all_to_all(routed, ("row", "col"), split_axis=0, concat_axis=0, tiled=True)
    (parts,) = expert_call([received], [device_count], [device_count], w_in, w_down, halves)
    returned = lax.all_to_all(parts, ("row", "col"), split_axis=0, concat_axis=0, tiled=True)
    if copies > 1:
        returned = returned.reshape(EXPERTS, copies, CAP, model_width).astype(jnp.float32)
        returned = jnp.sum(returned, axis=1).astype(jnp.bfloat16)
    returned = returned.reshape(EXPERTS * CAP, model_width)
    expert_sum = jnp.dot(place_gates, returned, preferred_element_type=jnp.float32)
    return (residual + expert_sum).astype(jnp.bfloat16)


def plane_places(expert_ids, gate_weights):
    row, col = lax.axis_index("row"), lax.axis_index("col")
    packed = jnp.concatenate(
        [expert_ids.astype(jnp.float32), gate_weights.astype(jnp.float32)], axis=1
    )
    one, two, three = [lax.ppermute(packed, "row", xor_pairs(4, bits)) for bits in (1, 2, 3)]
    outer = (row == 0) | (row == 3)
    packed = jnp.stack(
        [packed, one, jnp.where(outer, two, three), jnp.where(outer, three, two)]
    )
    top = expert_ids.shape[1]
    device = row * 8 + (col ^ jnp.arange(8, dtype=jnp.int32))
    experts = (device[:, None] * 2 + jnp.arange(2, dtype=jnp.int32)).reshape(-1)
    return slot_places(packed[..., :top].astype(jnp.int32), packed[..., top:], experts)


def experts_planes(moe_in, residual, places, gated, w_in, w_down):
    model_width = moe_in.shape[1]
    swap, middle, outward = xor_pairs(4, 1), [(1, 2), (2, 1)], [(1, 0), (2, 3)]
    inward = [(0, 1), (3, 2)]
    near = lax.ppermute(moe_in, "row", swap)
    cross = lax.ppermute(moe_in, "row", middle)
    cross_out = lax.ppermute(cross, "row", outward)
    far = lax.ppermute(near, "row", middle)
    far_out = lax.ppermute(far, "row", outward)

    def send(place, block):
        routed = route(place, block)
        chips = [routed[:64]]
        chips += [
            lax.ppermute(routed[64 * r : 64 * (r + 1)], "col", xor_pairs(8, 2 * r))
            for r in range(1, 4)
        ]
        return chips

    def share(chips):
        return jnp.concatenate([chip[32:] for chip in chips], axis=0)

    def swap_cores(rows):
        return lax.ppermute(rows, "col", xor_pairs(8, 1))

    def views(chips, other):
        return [chip.reshape(2, 2, CAP, model_width) for chip in chips] + [
            other.reshape(4, 2, CAP, model_width)
        ]

    chips_0 = send(places[0], moe_in)
    shared_0, near, cross = lax.optimization_barrier((share(chips_0), near, cross))
    other_0 = swap_cores(shared_0)
    chips_1 = send(places[1], near)
    shared_1, cross_out, far = lax.optimization_barrier((share(chips_1), cross_out, far))
    other_1 = swap_cores(shared_1)
    chips_2 = send(places[2], cross + cross_out)
    shared_2, far_out = lax.optimization_barrier((share(chips_2), far_out))
    other_2 = swap_cores(shared_2)
    chips_3 = send(places[3], far + far_out)
    other_3 = swap_cores(share(chips_3))

    def expert_parts(*blocks):
        xs = [view for chips, other in blocks for view in views(chips, other)]
        takes, outs = [1, 1, 1, 1, 4] * len(blocks), [4, 4] * len(blocks)
        return expert_call(xs, takes, outs, w_in, w_down, 2)

    parts = expert_parts(
        (chips_0, other_0), (chips_1, other_1), (chips_2, other_2), (chips_3, other_3)
    )

    def give_back(own, other, before=None):
        both = [
            jnp.concatenate([own[r].reshape(32, model_width), other[r].reshape(32, model_width)])
            for r in range(4)
        ]
        if before is not None:
            *both, unused = lax.optimization_barrier((*both, before[1]))
        return both[:1] + [
            lax.ppermute(both[r], "col", xor_pairs(8, 2 * r)) for r in range(1, 4)
        ]

    def combine(gates, chips):
        total = jnp.dot(gates[:, :64], chips[0], preferred_element_type=jnp.float32)
        for r in range(1, 4):
            total += jnp.dot(
                gates[:, 64 * r : 64 * (r + 1)], chips[r], preferred_element_type=jnp.float32
            )
        return total

    def narrow(total):
        return total.astype(jnp.bfloat16)

    back_3 = give_back(parts[6], swap_cores(parts[7]))
    back_2 = give_back(parts[4], swap_cores(parts[5]), back_3)
    sum_3 = narrow(combine(gated[3], back_3))
    ends = lax.ppermute(sum_3, "row", [(0, 3), (3, 0)])
    inner = lax.ppermute(sum_3, "row", [(1, 3), (2, 0)])
    back_1 = give_back(parts[2], swap_cores(parts[3]), back_2)
    sum_2 = combine(gated[2], back_2)
    hop = lax.ppermute(narrow(sum_2), "row", inward)
    back_0 = give_back(parts[0], swap_cores(parts[1]), back_1)
    beside = lax.ppermute(narrow(combine(gated[1], back_1)), "row", swap)
    middles = lax.ppermute(narrow(sum_2 + hop.astype(jnp.float32)), "row", middle)
    total = residual + combine(gated[0], back_0)
    for arrived in (ends, inner, beside, middles):
        total += arrived.astype(jnp.float32)
    return total.astype(jnp.bfloat16)


def body(
    hidden,
    cached_lengths,
    request_order,
    cache_keys,
    cache_values,
    attn_gain,
    w_qkv,
    w_out,
    moe_gain,
    expert_ids,
    gate_weights,
    w_in,
    w_down,
):
    tok_rows, model_width = hidden.shape
    heads_here = w_qkv.shape[1]
    row_count = lax.axis_size("row")
    col_count = lax.axis_size("col")
    device_count = row_count * col_count
    new_rows = tok_rows * col_count

    planes = row_count == 4 and col_count == 8 and w_in.shape[0] == 4

    normed = rms_scale(hidden, attn_gain).astype(jnp.bfloat16)
    if planes:
        slots, gated = plane_places(expert_ids, gate_weights)
        mine, other, w_out_late = gather_plane(normed, w_out)
        even_odd = [[0, 2, 4, 6], [1, 3, 5, 7]]
        w_out_mine = lax.all_gather(w_out_late, "col", axis=0, axis_index_groups=even_odd)
    else:
        gathered = lax.all_gather(normed, "col", axis=0, tiled=True)
        w_out_all = lax.all_gather(w_out, "col", axis=0)

    row_index = lax.axis_index("row")
    places = jnp.arange(request_order.shape[0], dtype=jnp.int32)
    request = jnp.sum(jnp.where(places == row_index, request_order, 0))
    length = jnp.sum(jnp.where(places == request, cached_lengths, 0))
    query_pos = length + jnp.arange(new_rows, dtype=jnp.int32)
    frequency = THETA ** (-2.0 * jnp.arange(HEAD // 2, dtype=jnp.float32) / HEAD)
    angles = query_pos.astype(jnp.float32)[:, None] * frequency
    cosine, sine = jnp.cos(angles), jnp.sin(angles)
    cosine = jnp.concatenate([cosine, cosine], axis=1)
    sine = jnp.concatenate([-sine, sine], axis=1)

    w_matrix = w_qkv.reshape(model_width, -1)
    if planes:
        col = lax.axis_index("col")
        chips = 2 * jnp.arange(4, dtype=jnp.int32)
        fresh = qkv_call(col ^ chips, mine, w_matrix, cosine, sine, heads_here)
        queries, new_keys, new_values = qkv_call(
            col ^ chips ^ 1, other, w_matrix, cosine, sine, heads_here, fresh
        )
    else:
        blocks = jnp.arange(col_count, dtype=jnp.int32)
        queries, new_keys, new_values = qkv_call(
            blocks, gathered, w_matrix, cosine, sine, heads_here
        )
    context = attention_call(
        length.reshape(1), queries, cache_keys, cache_values, new_keys, new_values
    )
    if planes:
        w_out_mine, context = lax.optimization_barrier((w_out_mine, context))
    shares = lax.all_to_all(
        context.reshape(col_count, tok_rows, heads_here * HEAD), "col", 0, 0, tiled=True
    )
    if planes:
        w_out_other = lax.ppermute(w_out_mine, "col", xor_pairs(8, 1))
        core = col & 1
        order = (chips[:, None] + jnp.stack([core, 1 - core])).reshape(-1)
        residual, moe_in = project_call(
            order, shares, [w_out_mine, w_out_other], hidden, moe_gain
        )
        new_hidden = experts_planes(moe_in, residual, slots, gated, w_in, w_down)
    else:
        residual, moe_in = project_call(blocks, shares, [w_out_all], hidden, moe_gain)
        new_hidden = experts_direct(moe_in, residual, expert_ids, gate_weights, w_in, w_down)
    return (new_hidden, new_keys, new_values)


def solution(mesh):
    in_specs = (
        P(("row", "col"), None),
        P(),
        P(),
        P("row", None, "col"),
        P("row", None, "col"),
        P(),
        P(None, "col", None),
        P("col", None),
        P(),
        P(("row", "col"), None),
        P(("row", "col"), None),
        P(("row", "col"), None, None),
        P(("row", "col"), None, None),
    )
    out_specs = (P(("row", "col"), None), P("row", "col"), P("row", "col"))
    return jax.shard_map(body, mesh=mesh, in_specs=in_specs, out_specs=out_specs, check_vma=False)
```

```python
import functools

import jax
import jax.numpy as jnp
from jax import lax
from jax.experimental import pallas as pl
from jax.experimental.pallas import tpu as pltpu
from jax.sharding import PartitionSpec as P

EXPERTS = 64
WINDOW = 4096
SINKS = 4
CAP = 16
HEAD = 128

EPS = 1e-06
THETA = 10000.0
LOG2E = 1.4426950408889634
NEG = -1e30
MIB = 1 << 20


def rms_scale(matrix, scaling):
    values = matrix.astype(jnp.float32)
    factor = lax.rsqrt(jnp.mean(values * values, axis=-1, keepdims=True) + EPS)
    return values * factor * scaling.astype(jnp.float32)


def qkv_kernel(heads, order_ref, x_ref, w_ref, cos_ref, sin_ref, *refs):
    q_ref, k_ref, v_ref = refs[-3:]
    projected = jnp.dot(x_ref[...], w_ref[...], preferred_element_type=jnp.float32)
    cosine = cos_ref[...]
    sine = sin_ref[...]
    for h in range(heads):
        base = h * 3 * HEAD
        out = slice(h * HEAD, (h + 1) * HEAD)
        q = projected[:, base : base + HEAD]
        k = projected[:, base + HEAD : base + 2 * HEAD]
        q = q * cosine + pltpu.roll(q, HEAD // 2, 1) * sine
        k = k * cosine + pltpu.roll(k, HEAD // 2, 1) * sine
        q_ref[:, out] = (q * (LOG2E * HEAD**-0.5)).astype(jnp.bfloat16)
        k_ref[:, out] = k.astype(jnp.bfloat16)
        v_ref[:, out] = projected[:, base + 2 * HEAD : base + 3 * HEAD].astype(jnp.bfloat16)


def qkv_call(order, x, w, cosine, sine, heads, before=()):
    rows, width = x.shape
    total = cosine.shape[0]
    block = rows // order.shape[0]
    out = jax.ShapeDtypeStruct((total, heads * HEAD), jnp.bfloat16)
    placed = lambda i, n: (n[i], 0)
    out_spec = pl.BlockSpec((block, heads * HEAD), placed)
    return pl.pallas_call(
        functools.partial(qkv_kernel, heads),
        grid_spec=pltpu.PrefetchScalarGridSpec(
            num_scalar_prefetch=1,
            grid=(rows // block,),
            in_specs=[
                pl.BlockSpec((block, width), lambda i, n: (i, 0)),
                pl.BlockSpec(w.shape, lambda i, n: (0, 0)),
                pl.BlockSpec((block, HEAD), placed),
                pl.BlockSpec((block, HEAD), placed),
            ]
            + [pl.BlockSpec(memory_space=pl.ANY)] * len(before),
            out_specs=[out_spec] * 3,
        ),
        out_shape=[out] * 3,
        input_output_aliases={5 + i: i for i in range(len(before))},
        compiler_params=pltpu.CompilerParams(vmem_limit_bytes=24 * MIB),
        cost_estimate=pl.CostEstimate(
            flops=2 * rows * width * w.shape[1],
            bytes_accessed=2 * (rows * width + w.size + 3 * rows * heads * HEAD),
            transcendentals=0,
        ),
        name="qkv",
    )(order, x, w, cosine, sine, *before)


def attention_kernel(heads, bq, bk, info_ref, q_ref, kc_ref, vc_ref, kn_ref, vn_ref, o_ref, *scores):
    length, flip = info_ref[0], info_ref[1]
    cache_rows, new_rows = kc_ref.shape[1], kn_ref.shape[0]
    q_start = pl.program_id(0) * bq
    first = length + q_start
    last = first + bq - 1
    blocks = (length + bk - 1) // bk
    lowest = jnp.maximum(first - WINDOW + 1, 0) // bk
    inside = jnp.minimum((jnp.maximum(last - WINDOW + 1, 0) + bk - 1) // bk, blocks)
    whole = jnp.maximum(inside, length // bk)

    def rows_and_places(size):
        return (
            lax.broadcasted_iota(jnp.int32, (bq, size), 0),
            lax.broadcasted_iota(jnp.int32, (bq, size), 1),
        )

    def walk(visit, state):
        def cached(start, size):
            def load(ref, h):
                return ref[0, pl.ds(start, size), h * HEAD : (h + 1) * HEAD]

            return functools.partial(load, kc_ref), functools.partial(load, vc_ref)

        def fresh(start, size):
            def load(ref, h):
                return ref[pl.ds(start, size), h * HEAD : (h + 1) * HEAD]

            return functools.partial(load, kn_ref), functools.partial(load, vn_ref)

        def sink_step(j, state):
            def allowed():
                rows, places = rows_and_places(HEAD)
                out_of_window = first + rows - places >= WINDOW
                return (places < SINKS) & (places < lowest * bk) & out_of_window

            return visit(state, *cached(0, HEAD), allowed, cache_rows + new_rows, HEAD)

        def masked_step(j, state):
            start = pl.multiple_of(j * bk, bk)

            def allowed():
                rows, places = rows_and_places(bk)
                places = start + places
                in_window = first + rows - places < WINDOW
                return (places < length) & (in_window | (places < SINKS))

            return visit(state, *cached(start, bk), allowed, start, bk)

        def plain_step(j, state):
            start = pl.multiple_of(j * bk, bk)
            return visit(state, *cached(start, bk), None, start, bk)

        def fresh_step(j, state):
            start = pl.multiple_of(j * bq, bq)
            slot = pl.multiple_of(cache_rows + start, bq)
            return visit(state, *fresh(start, bq), None, slot, bq)

        def causal():
            rows, places = rows_and_places(bq)
            return places <= rows

        state = lax.fori_loop(0, jnp.minimum(lowest, 1), sink_step, state)
        state = lax.fori_loop(lowest, inside, masked_step, state)
        state = lax.fori_loop(inside, whole, plain_step, state)
        state = lax.fori_loop(whole, blocks, masked_step, state)
        state = lax.fori_loop(0, pl.program_id(0), fresh_step, state)
        start = pl.multiple_of(q_start, bq)
        slot = pl.multiple_of(cache_rows + q_start, bq)
        return visit(state, *fresh(start, bq), causal, slot, bq)

    def score(state, keys, values, allowed, slot, size):
        allowed = None if allowed is None else allowed()
        new_state = []
        for h in range(heads):
            s = lax.dot_general(
                q_ref[:, h * HEAD : (h + 1) * HEAD],
                keys(h),
                (((1,), (1,)), ((), ())),
                preferred_element_type=jnp.float32,
            )
            if allowed is not None:
                s = jnp.where(allowed, s, NEG)
            scores[h][:, pl.ds(slot, size)] = s
            highest = state[h]
            for c in range(0, size, HEAD):
                highest = jnp.maximum(highest, s[:, c : c + HEAD])
            new_state.append(highest)
        return tuple(new_state)

    highest = walk(score, (jnp.full((bq, HEAD), NEG, jnp.float32),) * heads)
    highest = [jnp.max(part, axis=1, keepdims=True) for part in highest]

    def weigh(state, keys, values, allowed, slot, size):
        new_state = []
        for h in range(heads):
            p = jnp.exp2(scores[h][:, pl.ds(slot, size)] - highest[h]).astype(jnp.bfloat16)
            v = values(h)
            v = jnp.concatenate([v, jnp.ones_like(v)], axis=1)
            new_state.append(state[h] + jnp.dot(p, v, preferred_element_type=jnp.float32))
        return tuple(new_state)

    sums = walk(weigh, (jnp.zeros((bq, 2 * HEAD), jnp.float32),) * heads)
    tokens = o_ref.shape[1]
    for h in range(heads):
        out = (sums[h][:, :HEAD] / sums[h][:, HEAD:]).astype(o_ref.dtype)
        for j in range(bq // tokens):
            place = (pl.program_id(0) * (bq // tokens) + j) ^ flip
            o_ref[place, :, h * HEAD : (h + 1) * HEAD] = out[j * tokens : (j + 1) * tokens]


def attention_call(length, flip, tokens, q, cache_keys, cache_values, new_keys, new_values):
    rows, width = q.shape
    heads = width // HEAD
    cache_rows = cache_keys.shape[1]
    bq, bk = min(512, rows), min(1024, cache_rows)
    fixed = lambda shape: pl.BlockSpec(shape, lambda i, n: (0,) * len(shape))
    out_shape = (rows // tokens, tokens, width)
    return pl.pallas_call(
        functools.partial(attention_kernel, heads, bq, bk),
        grid_spec=pltpu.PrefetchScalarGridSpec(
            num_scalar_prefetch=1,
            grid=(rows // bq,),
            in_specs=[
                pl.BlockSpec((bq, width), lambda i, n: (i, 0)),
                fixed(cache_keys.shape),
                fixed(cache_values.shape),
                fixed(new_keys.shape),
                fixed(new_values.shape),
            ],
            out_specs=fixed(out_shape),
            scratch_shapes=[pltpu.VMEM((bq, cache_rows + rows + HEAD), jnp.float32)] * heads,
        ),
        out_shape=jax.ShapeDtypeStruct(out_shape, jnp.bfloat16),
        compiler_params=pltpu.CompilerParams(vmem_limit_bytes=50 * MIB),
        cost_estimate=pl.CostEstimate(
            flops=4 * rows * width * (cache_rows + rows),
            bytes_accessed=4 * (cache_rows + 2 * rows) * width,
            transcendentals=rows * heads * (cache_rows + rows),
        ),
        name="attention",
    )(jnp.stack([length, flip]), q, cache_keys, cache_values, new_keys, new_values)


def project_kernel(parts, order_ref, *refs):
    x_refs, w_refs = refs[:parts], refs[parts : 2 * parts]
    hidden_ref, gain_ref, resid_ref, normed_ref = refs[2 * parts :]
    g = pl.program_id(0)

    @pl.when(g == 0)
    def _():
        resid_ref[...] = hidden_ref[...].astype(jnp.float32)

    for x_ref, w_ref in zip(x_refs, w_refs):
        share = jnp.dot(x_ref[0], w_ref[0], preferred_element_type=jnp.float32)
        resid_ref[...] += share.astype(jnp.bfloat16).astype(jnp.float32)

    @pl.when(g == pl.num_programs(0) - 1)
    def _():
        normed_ref[...] = rms_scale(resid_ref[...], gain_ref[...]).astype(jnp.bfloat16)


def project_call(order, xs, weights, hidden, gain):
    parts = len(weights)
    steps, rows, width = xs[0].shape
    model = weights[0].shape[2]
    fixed = pl.BlockSpec((rows, model), lambda g, n: (0, 0))
    return pl.pallas_call(
        functools.partial(project_kernel, parts),
        grid_spec=pltpu.PrefetchScalarGridSpec(
            num_scalar_prefetch=1,
            grid=(steps,),
            in_specs=[pl.BlockSpec((1, rows, width), lambda g, n: (g, 0, 0))] * parts
            + [pl.BlockSpec((1, width, model), lambda g, n: (n[g], 0, 0))] * parts
            + [fixed, pl.BlockSpec((1, model), lambda g, n: (0, 0))],
            out_specs=[fixed, fixed],
        ),
        out_shape=[
            jax.ShapeDtypeStruct((rows, model), jnp.float32),
            jax.ShapeDtypeStruct((rows, model), jnp.bfloat16),
        ],
        compiler_params=pltpu.CompilerParams(vmem_limit_bytes=24 * MIB),
        cost_estimate=pl.CostEstimate(
            flops=2 * rows * model * steps * parts * width,
            bytes_accessed=2 * steps * parts * (width * model + rows * width) + 8 * rows * model,
            transcendentals=0,
        ),
        name="project",
    )(order, *xs, *weights, hidden, gain.reshape(1, model))


def share_kernel(order_ref, x_ref, w_ref, here_ref, beside_ref):
    tokens = here_ref.shape[0]
    x = x_ref[0].reshape(2 * tokens, x_ref.shape[3])
    share = jnp.dot(x, w_ref[0], preferred_element_type=jnp.float32)
    share = share.astype(jnp.bfloat16).astype(jnp.float32)

    @pl.when(pl.program_id(0) == 0)
    def _():
        here_ref[...] = share[:tokens]
        beside_ref[...] = share[tokens:]

    @pl.when(pl.program_id(0) > 0)
    def _():
        here_ref[...] += share[:tokens]
        beside_ref[...] += share[tokens:]


def share_call(order, x, weight):
    steps, unused, tokens, width = x.shape
    model = weight.shape[2]
    fixed = pl.BlockSpec((tokens, model), lambda g, n: (0, 0))
    return pl.pallas_call(
        share_kernel,
        grid_spec=pltpu.PrefetchScalarGridSpec(
            num_scalar_prefetch=1,
            grid=(steps,),
            in_specs=[
                pl.BlockSpec((1, 2, tokens, width), lambda g, n: (g, 0, 0, 0)),
                pl.BlockSpec((1, width, model), lambda g, n: (n[g], 0, 0)),
            ],
            out_specs=[fixed] * 2,
        ),
        out_shape=[jax.ShapeDtypeStruct((tokens, model), jnp.float32)] * 2,
        compiler_params=pltpu.CompilerParams(vmem_limit_bytes=24 * MIB),
        cost_estimate=pl.CostEstimate(
            flops=4 * tokens * model * steps * width,
            bytes_accessed=2 * steps * width * model + 8 * tokens * model,
            transcendentals=0,
        ),
        name="share",
    )(order, x, weight)


def norm_kernel(hidden_ref, here_ref, beside_ref, gain_ref, resid_ref, normed_ref):
    resid = hidden_ref[...].astype(jnp.float32) + here_ref[...] + beside_ref[...]
    resid_ref[...] = resid
    normed_ref[...] = rms_scale(resid, gain_ref[...]).astype(jnp.bfloat16)


def norm_call(hidden, here, beside, gain):
    return pl.pallas_call(
        norm_kernel,
        out_shape=[
            jax.ShapeDtypeStruct(hidden.shape, jnp.float32),
            jax.ShapeDtypeStruct(hidden.shape, jnp.bfloat16),
        ],
        compiler_params=pltpu.CompilerParams(vmem_limit_bytes=16 * MIB),
        cost_estimate=pl.CostEstimate(
            flops=8 * hidden.size, bytes_accessed=16 * hidden.size, transcendentals=0
        ),
        name="norm",
    )(hidden, here, beside, gain.reshape(1, -1))


def expert_kernel(half, counts, resident, *refs):
    x_refs = refs[: len(counts)]
    win_ref, wdown_ref = refs[len(counts) : len(counts) + 2]
    o_refs, acc_ref = refs[len(counts) + 2 : -1], refs[-1]
    h = pl.program_id(1)
    width = x_refs[0].shape[-1]
    x = [ref[...].reshape(-1, width) for ref in x_refs]
    x = x[0] if len(x) == 1 else jnp.concatenate(x, axis=0)
    at = pl.program_id(0) * pl.num_programs(1) + h if resident else 0
    both = jnp.dot(x, win_ref[at], preferred_element_type=jnp.float32)
    a = both[:, :half]
    b = both[:, half:]
    act = (a / (1.0 + jnp.exp(-a)) * b).astype(jnp.bfloat16)
    part = jnp.dot(act, wdown_ref[0], preferred_element_type=jnp.float32)

    @pl.when(h == 0)
    def _():
        acc_ref[...] = part

    @pl.when(h > 0)
    def _():
        acc_ref[...] += part

    @pl.when(h == pl.num_programs(1) - 1)
    def _():
        start = 0
        for ref in o_refs:
            size = ref.shape[0] * ref.shape[2]
            ref[...] = acc_ref[start : start + size].astype(jnp.bfloat16).reshape(ref.shape)
            start += size


def expert_call(xs, takes, outs, w_in, w_down, halves, resident=False):
    unused, unused, slots, width = xs[0].shape
    experts = w_in.shape[0] // halves
    units, model = w_down.shape[1:]
    rows = sum(takes) * slots
    block = lambda senders: pl.BlockSpec((senders, 1, slots, width), lambda e, h: (0, e, 0, 0))
    weight_specs = [
        pl.BlockSpec((1, width, 2 * units), lambda e, h: (e * halves + h, 0, 0)),
        pl.BlockSpec((1, units, model), lambda e, h: (e * halves + h, 0, 0)),
    ]
    if resident:
        weight_specs[0] = pl.BlockSpec(memory_space=pltpu.VMEM)
    return pl.pallas_call(
        functools.partial(expert_kernel, units, takes, resident),
        grid=(experts, halves),
        in_specs=[block(senders) for senders in takes] + weight_specs,
        out_specs=[block(senders) for senders in outs],
        out_shape=[
            jax.ShapeDtypeStruct((senders, experts, slots, width), jnp.bfloat16) for senders in outs
        ],
        scratch_shapes=[pltpu.VMEM((rows, model), jnp.float32)],
        compiler_params=pltpu.CompilerParams(vmem_limit_bytes=(24 if resident else 56) * MIB),
        cost_estimate=pl.CostEstimate(
            flops=6 * rows * experts * halves * width * units,
            bytes_accessed=2 * (w_in.size + w_down.size + 2 * rows * experts * width),
            transcendentals=rows * experts * halves * units,
        ),
        name="experts",
    )(*xs, w_in, w_down)


def xor_pairs(count, bits):
    return [(i, i ^ bits) for i in range(count)]


def gather_plane(block, later):
    rows = block.shape[0]
    along_x = lax.ppermute(block, "col", xor_pairs(8, 2))
    along_y = lax.ppermute(block, "col", xor_pairs(8, 4))
    along_x, along_y, later = lax.optimization_barrier((along_x, along_y, later))
    across_0 = lax.ppermute(along_x[: rows // 2], "col", xor_pairs(8, 4))
    across_1 = lax.ppermute(along_y[rows // 2 :], "col", xor_pairs(8, 2))
    mine = jnp.concatenate([block, along_x, along_y, across_0, across_1], axis=0)
    return mine, lax.ppermute(mine, "col", xor_pairs(8, 1)), later


def slot_places(ids, gates, experts):
    rows = ids.shape[-2]
    chosen = ids[..., None] == experts
    named = jnp.any(chosen, axis=-2)
    weight = jnp.sum(jnp.where(chosen, gates[..., None], 0.0), axis=-2)
    earlier = jnp.arange(rows)[:, None] > jnp.arange(rows)[None, :]
    rank = jnp.einsum(
        "ij,...je->...ie",
        earlier.astype(jnp.bfloat16),
        named.astype(jnp.bfloat16),
        preferred_element_type=jnp.float32,
    ).astype(jnp.int32)
    rank = jnp.where(named, rank, -1)
    place = rank[..., None] == jnp.arange(CAP, dtype=jnp.int32)
    gated = jnp.where(place, weight[..., None], 0.0).astype(jnp.bfloat16)
    flat = ids.shape[:-1] + (experts.shape[0] * CAP,)
    return place.reshape(flat).astype(jnp.bfloat16), gated.reshape(flat)


def route(place, rows):
    return lax.dot_general(
        place, rows, (((0,), (0,)), ((), ())), preferred_element_type=jnp.float32
    ).astype(jnp.bfloat16)


def experts_direct(moe_in, residual, expert_ids, gate_weights, w_in, w_down):
    tok_rows, model_width = moe_in.shape
    device_count = lax.axis_size("row") * lax.axis_size("col")
    place, place_gates = slot_places(
        expert_ids, gate_weights.astype(jnp.float32), jnp.arange(EXPERTS, dtype=jnp.int32)
    )
    per_device = w_in.shape[0]
    halves = 2 if per_device % 2 == 0 else 1
    copies = 2 // halves
    routed = route(place, moe_in).reshape(EXPERTS, 1, CAP, model_width)
    routed = jnp.broadcast_to(routed, (EXPERTS, copies, CAP, model_width))
    routed = routed.reshape(device_count, per_device // halves, CAP, model_width)
    received = lax.all_to_all(routed, ("row", "col"), split_axis=0, concat_axis=0, tiled=True)
    (parts,) = expert_call([received], [device_count], [device_count], w_in, w_down, halves)
    returned = lax.all_to_all(parts, ("row", "col"), split_axis=0, concat_axis=0, tiled=True)
    if copies > 1:
        returned = returned.reshape(EXPERTS, copies, CAP, model_width).astype(jnp.float32)
        returned = jnp.sum(returned, axis=1).astype(jnp.bfloat16)
    returned = returned.reshape(EXPERTS * CAP, model_width)
    expert_sum = jnp.dot(place_gates, returned, preferred_element_type=jnp.float32)
    return (residual + expert_sum).astype(jnp.bfloat16)


def plane_places(expert_ids, gate_weights):
    row, col = lax.axis_index("row"), lax.axis_index("col")
    packed = jnp.concatenate(
        [expert_ids.astype(jnp.float32), gate_weights.astype(jnp.float32)], axis=1
    )
    one, two, three = [lax.ppermute(packed, "row", xor_pairs(4, bits)) for bits in (1, 2, 3)]
    outer = (row == 0) | (row == 3)
    packed = jnp.stack(
        [packed, one, jnp.where(outer, two, three), jnp.where(outer, three, two)]
    )
    top = expert_ids.shape[1]
    device = row * 8 + (col ^ jnp.arange(8, dtype=jnp.int32))
    experts = (device[:, None] * 2 + jnp.arange(2, dtype=jnp.int32)).reshape(-1)
    return slot_places(packed[..., :top].astype(jnp.int32), packed[..., top:], experts)


def experts_planes(moe_in, residual, places, gated, w_in, w_down):
    model_width = moe_in.shape[1]
    swap, middle, outward = xor_pairs(4, 1), [(1, 2), (2, 1)], [(1, 0), (2, 3)]
    inward = [(0, 1), (3, 2)]
    near = lax.ppermute(moe_in, "row", swap)
    cross = lax.ppermute(moe_in, "row", middle)
    cross_out = lax.ppermute(cross, "row", outward)
    far = lax.ppermute(near, "row", middle)
    far_out = lax.ppermute(far, "row", outward)

    def send(routed):
        chips = [routed[:64]]
        chips += [
            lax.ppermute(routed[64 * r : 64 * (r + 1)], "col", xor_pairs(8, 2 * r))
            for r in range(1, 4)
        ]
        return chips

    def share(chips):
        return jnp.concatenate([chip[32:] for chip in chips], axis=0)

    def swap_cores(rows):
        return lax.ppermute(rows, "col", xor_pairs(8, 1))

    def views(chips, other):
        return [chip.reshape(2, 2, CAP, model_width) for chip in chips] + [
            other.reshape(4, 2, CAP, model_width)
        ]

    chips_0 = send(route(places[0], moe_in))
    routed_1 = route(places[1], near)
    shared_0, routed_1, cross = lax.optimization_barrier((share(chips_0), routed_1, cross))
    other_0 = swap_cores(shared_0)
    chips_1 = send(routed_1)
    routed_2 = route(places[2], cross + cross_out)
    shared_1, routed_2, far = lax.optimization_barrier((share(chips_1), routed_2, far))
    other_1 = swap_cores(shared_1)
    chips_2 = send(routed_2)
    routed_3 = route(places[3], far + far_out)
    shared_2, routed_3 = lax.optimization_barrier((share(chips_2), routed_3))
    other_2 = swap_cores(shared_2)
    chips_3 = send(routed_3)
    other_3 = swap_cores(share(chips_3))

    def expert_parts(*blocks):
        xs = [view for chips, other in blocks for view in views(chips, other)]
        takes, outs = [1, 1, 1, 1, 4] * len(blocks), [4, 4] * len(blocks)
        return expert_call(xs, takes, outs, w_in, w_down, 2)

    parts = expert_parts(
        (chips_0, other_0), (chips_1, other_1), (chips_2, other_2), (chips_3, other_3)
    )

    def give_back(own, other, before=None):
        both = [
            jnp.concatenate([own[r].reshape(32, model_width), other[r].reshape(32, model_width)])
            for r in range(4)
        ]
        if before is not None:
            *both, unused = lax.optimization_barrier((*both, before[1]))
        return both[:1] + [
            lax.ppermute(both[r], "col", xor_pairs(8, 2 * r)) for r in range(1, 4)
        ]

    def combine(gates, chips):
        total = jnp.dot(gates[:, :64], chips[0], preferred_element_type=jnp.float32)
        for r in range(1, 4):
            total += jnp.dot(
                gates[:, 64 * r : 64 * (r + 1)], chips[r], preferred_element_type=jnp.float32
            )
        return total

    def narrow(total):
        return total.astype(jnp.bfloat16)

    back_2 = give_back(parts[4], swap_cores(parts[5]))
    back_3 = give_back(parts[6], swap_cores(parts[7]), back_2)
    sum_2 = combine(gated[2], back_2)
    hop = lax.ppermute(narrow(sum_2), "row", inward)
    back_1 = give_back(parts[2], swap_cores(parts[3]), back_3)
    sum_3 = narrow(combine(gated[3], back_3))
    ends = lax.ppermute(sum_3, "row", [(0, 3), (3, 0)])
    inner = lax.ppermute(sum_3, "row", [(1, 3), (2, 0)])
    back_0 = give_back(parts[0], swap_cores(parts[1]), back_1)
    middles = lax.ppermute(narrow(sum_2 + hop.astype(jnp.float32)), "row", middle)
    beside = lax.ppermute(narrow(combine(gated[1], back_1)), "row", swap)
    total = residual + combine(gated[0], back_0)
    for arrived in (ends, inner, beside, middles):
        total += arrived.astype(jnp.float32)
    return total.astype(jnp.bfloat16)


def body(
    hidden,
    cached_lengths,
    request_order,
    cache_keys,
    cache_values,
    attn_gain,
    w_qkv,
    w_out,
    moe_gain,
    expert_ids,
    gate_weights,
    w_in,
    w_down,
):
    tok_rows, model_width = hidden.shape
    heads_here = w_qkv.shape[1]
    row_count = lax.axis_size("row")
    col_count = lax.axis_size("col")
    device_count = row_count * col_count
    new_rows = tok_rows * col_count

    planes = row_count == 4 and col_count == 8 and w_in.shape[0] == 4

    row_index = lax.axis_index("row")
    places = jnp.arange(request_order.shape[0], dtype=jnp.int32)
    request = jnp.sum(jnp.where(places == row_index, request_order, 0))
    length = jnp.sum(jnp.where(places == request, cached_lengths, 0))
    query_pos = length + jnp.arange(new_rows, dtype=jnp.int32)
    frequency = THETA ** (-2.0 * jnp.arange(HEAD // 2, dtype=jnp.float32) / HEAD)
    angles = query_pos.astype(jnp.float32)[:, None] * frequency
    cosine, sine = jnp.cos(angles), jnp.sin(angles)
    cosine = jnp.concatenate([cosine, cosine], axis=1)
    sine = jnp.concatenate([-sine, sine], axis=1)

    w_matrix = w_qkv.reshape(model_width, -1)
    normed = rms_scale(hidden, attn_gain).astype(jnp.bfloat16)
    if planes:
        col = lax.axis_index("col")
        chips = jnp.arange(4, dtype=jnp.int32)
        slots, gated = plane_places(expert_ids, gate_weights)
        mine, other, w_out_late = gather_plane(normed, w_out)
        even_odd = [[0, 2, 4, 6], [1, 3, 5, 7]]
        w_out_mine = lax.all_gather(w_out_late, "col", axis=0, axis_index_groups=even_odd)
        fresh = qkv_call(col ^ 2 * chips, mine, w_matrix, cosine, sine, heads_here)
        queries, new_keys, new_values = qkv_call(
            col ^ 2 * chips ^ 1, other, w_matrix, cosine, sine, heads_here, fresh
        )
        context = attention_call(
            length, col, tok_rows, queries, cache_keys, cache_values, new_keys, new_values
        )
        arrived = [context[:2]] + [
            lax.ppermute(context[2 * r : 2 * r + 2], "col", xor_pairs(8, 2 * r))
            for r in range(1, 4)
        ]
        here, beside = share_call((col >> 1) ^ chips, jnp.stack(arrived), w_out_mine)
        beside = lax.ppermute(beside, "col", xor_pairs(8, 1))
        residual, moe_in = norm_call(hidden, here, beside, moe_gain)
        new_hidden = experts_planes(moe_in, residual, slots, gated, w_in, w_down)
    else:
        gathered = lax.all_gather(normed, "col", axis=0, tiled=True)
        w_out_all = lax.all_gather(w_out, "col", axis=0)
        blocks = jnp.arange(col_count, dtype=jnp.int32)
        queries, new_keys, new_values = qkv_call(
            blocks, gathered, w_matrix, cosine, sine, heads_here
        )
        context = attention_call(
            length,
            jnp.int32(0),
            tok_rows,
            queries,
            cache_keys,
            cache_values,
            new_keys,
            new_values,
        )
        shares = lax.all_to_all(context, "col", 0, 0, tiled=True)
        residual, moe_in = project_call(blocks, [shares], [w_out_all], hidden, moe_gain)
        new_hidden = experts_direct(moe_in, residual, expert_ids, gate_weights, w_in, w_down)
    return (new_hidden, new_keys, new_values)


def solution(mesh):
    in_specs = (
        P(("row", "col"), None),
        P(),
        P(),
        P("row", None, "col"),
        P("row", None, "col"),
        P(),
        P(None, "col", None),
        P("col", None),
        P(),
        P(("row", "col"), None),
        P(("row", "col"), None),
        P(("row", "col"), None, None),
        P(("row", "col"), None, None),
    )
    out_specs = (P(("row", "col"), None), P("row", "col"), P("row", "col"))
    return jax.shard_map(body, mesh=mesh, in_specs=in_specs, out_specs=out_specs, check_vma=False)
```

```python
import functools

import jax
import jax.numpy as jnp
from jax import lax
from jax.experimental import pallas as pl
from jax.experimental.pallas import tpu as pltpu
from jax.sharding import PartitionSpec as P

EXPERTS = 64
WINDOW = 4096
SINKS = 4
CAP = 16
HEAD = 128

EPS = 1e-06
THETA = 10000.0
LOG2E = 1.4426950408889634
NEG = -1e30
MIB = 1 << 20


def rms_scale(matrix, scaling):
    values = matrix.astype(jnp.float32)
    factor = lax.rsqrt(jnp.mean(values * values, axis=-1, keepdims=True) + EPS)
    return values * factor * scaling.astype(jnp.float32)


def qkv_kernel(heads, order_ref, x_ref, w_ref, cos_ref, sin_ref, *refs):
    q_ref, k_ref, v_ref = refs[-3:]
    projected = jnp.dot(x_ref[...], w_ref[...], preferred_element_type=jnp.float32)
    cosine = cos_ref[...]
    sine = sin_ref[...]
    for h in range(heads):
        base = h * 3 * HEAD
        out = slice(h * HEAD, (h + 1) * HEAD)
        q = projected[:, base : base + HEAD]
        k = projected[:, base + HEAD : base + 2 * HEAD]
        q = q * cosine + pltpu.roll(q, HEAD // 2, 1) * sine
        k = k * cosine + pltpu.roll(k, HEAD // 2, 1) * sine
        q_ref[:, out] = (q * (LOG2E * HEAD**-0.5)).astype(jnp.bfloat16)
        k_ref[:, out] = k.astype(jnp.bfloat16)
        v_ref[:, out] = projected[:, base + 2 * HEAD : base + 3 * HEAD].astype(jnp.bfloat16)


def qkv_call(order, x, w, cosine, sine, heads, before=()):
    rows, width = x.shape
    total = cosine.shape[0]
    block = rows // order.shape[0]
    out = jax.ShapeDtypeStruct((total, heads * HEAD), jnp.bfloat16)
    placed = lambda i, n: (n[i], 0)
    out_spec = pl.BlockSpec((block, heads * HEAD), placed)
    return pl.pallas_call(
        functools.partial(qkv_kernel, heads),
        grid_spec=pltpu.PrefetchScalarGridSpec(
            num_scalar_prefetch=1,
            grid=(rows // block,),
            in_specs=[
                pl.BlockSpec((block, width), lambda i, n: (i, 0)),
                pl.BlockSpec(w.shape, lambda i, n: (0, 0)),
                pl.BlockSpec((block, HEAD), placed),
                pl.BlockSpec((block, HEAD), placed),
            ]
            + [pl.BlockSpec(memory_space=pl.ANY)] * len(before),
            out_specs=[out_spec] * 3,
        ),
        out_shape=[out] * 3,
        input_output_aliases={5 + i: i for i in range(len(before))},
        compiler_params=pltpu.CompilerParams(vmem_limit_bytes=24 * MIB),
        cost_estimate=pl.CostEstimate(
            flops=2 * rows * width * w.shape[1],
            bytes_accessed=2 * (rows * width + w.size + 3 * rows * heads * HEAD),
            transcendentals=0,
        ),
        name="qkv",
    )(order, x, w, cosine, sine, *before)


def attention_kernel(heads, bq, bk, info_ref, q_ref, kc_ref, vc_ref, kn_ref, vn_ref, o_ref, *scores):
    length, flip = info_ref[0], info_ref[1]
    cache_rows, new_rows = kc_ref.shape[1], kn_ref.shape[0]
    q_start = pl.program_id(0) * bq
    first = length + q_start
    last = first + bq - 1
    blocks = (length + bk - 1) // bk
    lowest = jnp.maximum(first - WINDOW + 1, 0) // bk
    inside = jnp.minimum((jnp.maximum(last - WINDOW + 1, 0) + bk - 1) // bk, blocks)
    whole = jnp.maximum(inside, length // bk)

    def rows_and_places(size):
        return (
            lax.broadcasted_iota(jnp.int32, (bq, size), 0),
            lax.broadcasted_iota(jnp.int32, (bq, size), 1),
        )

    def walk(visit, state):
        def cached(start, size):
            def load(ref, h):
                return ref[0, pl.ds(start, size), h * HEAD : (h + 1) * HEAD]

            return functools.partial(load, kc_ref), functools.partial(load, vc_ref)

        def fresh(start, size):
            def load(ref, h):
                return ref[pl.ds(start, size), h * HEAD : (h + 1) * HEAD]

            return functools.partial(load, kn_ref), functools.partial(load, vn_ref)

        def sink_step(j, state):
            def allowed():
                rows, places = rows_and_places(HEAD)
                out_of_window = first + rows - places >= WINDOW
                return (places < SINKS) & (places < lowest * bk) & out_of_window

            return visit(state, *cached(0, HEAD), allowed, cache_rows + new_rows, HEAD)

        def masked_step(j, state):
            start = pl.multiple_of(j * bk, bk)

            def allowed():
                rows, places = rows_and_places(bk)
                places = start + places
                in_window = first + rows - places < WINDOW
                return (places < length) & (in_window | (places < SINKS))

            return visit(state, *cached(start, bk), allowed, start, bk)

        def plain_step(j, state):
            start = pl.multiple_of(j * bk, bk)
            return visit(state, *cached(start, bk), None, start, bk)

        def fresh_step(j, state):
            start = pl.multiple_of(j * bq, bq)
            slot = pl.multiple_of(cache_rows + start, bq)
            return visit(state, *fresh(start, bq), None, slot, bq)

        def causal():
            rows, places = rows_and_places(bq)
            return places <= rows

        state = lax.fori_loop(0, jnp.minimum(lowest, 1), sink_step, state)
        state = lax.fori_loop(lowest, inside, masked_step, state)
        state = lax.fori_loop(inside, whole, plain_step, state)
        state = lax.fori_loop(whole, blocks, masked_step, state)
        state = lax.fori_loop(0, pl.program_id(0), fresh_step, state)
        start = pl.multiple_of(q_start, bq)
        slot = pl.multiple_of(cache_rows + q_start, bq)
        return visit(state, *fresh(start, bq), causal, slot, bq)

    def score(state, keys, values, allowed, slot, size):
        allowed = None if allowed is None else allowed()
        new_state = []
        for h in range(heads):
            s = lax.dot_general(
                q_ref[:, h * HEAD : (h + 1) * HEAD],
                keys(h),
                (((1,), (1,)), ((), ())),
                preferred_element_type=jnp.float32,
            )
            if allowed is not None:
                s = jnp.where(allowed, s, NEG)
            scores[h][:, pl.ds(slot, size)] = s
            highest = state[h]
            for c in range(0, size, HEAD):
                highest = jnp.maximum(highest, s[:, c : c + HEAD])
            new_state.append(highest)
        return tuple(new_state)

    highest = walk(score, (jnp.full((bq, HEAD), NEG, jnp.float32),) * heads)
    highest = [jnp.max(part, axis=1, keepdims=True) for part in highest]

    def weigh(state, keys, values, allowed, slot, size):
        new_state = []
        for h in range(heads):
            p = jnp.exp2(scores[h][:, pl.ds(slot, size)] - highest[h]).astype(jnp.bfloat16)
            v = values(h)
            v = jnp.concatenate([v, jnp.ones_like(v)], axis=1)
            new_state.append(state[h] + jnp.dot(p, v, preferred_element_type=jnp.float32))
        return tuple(new_state)

    sums = walk(weigh, (jnp.zeros((bq, 2 * HEAD), jnp.float32),) * heads)
    tokens = o_ref.shape[1]
    for h in range(heads):
        out = (sums[h][:, :HEAD] / sums[h][:, HEAD:]).astype(o_ref.dtype)
        for j in range(bq // tokens):
            place = (pl.program_id(0) * (bq // tokens) + j) ^ flip
            o_ref[place, :, h * HEAD : (h + 1) * HEAD] = out[j * tokens : (j + 1) * tokens]


def attention_call(length, flip, tokens, q, cache_keys, cache_values, new_keys, new_values):
    rows, width = q.shape
    heads = width // HEAD
    cache_rows = cache_keys.shape[1]
    bq, bk = min(512, rows), min(2048, cache_rows)
    fixed = lambda shape: pl.BlockSpec(shape, lambda i, n: (0,) * len(shape))
    out_shape = (rows // tokens, tokens, width)
    return pl.pallas_call(
        functools.partial(attention_kernel, heads, bq, bk),
        grid_spec=pltpu.PrefetchScalarGridSpec(
            num_scalar_prefetch=1,
            grid=(rows // bq,),
            in_specs=[
                pl.BlockSpec((bq, width), lambda i, n: (i, 0)),
                fixed(cache_keys.shape),
                fixed(cache_values.shape),
                fixed(new_keys.shape),
                fixed(new_values.shape),
            ],
            out_specs=fixed(out_shape),
            scratch_shapes=[pltpu.VMEM((bq, cache_rows + rows + HEAD), jnp.float32)] * heads,
        ),
        out_shape=jax.ShapeDtypeStruct(out_shape, jnp.bfloat16),
        compiler_params=pltpu.CompilerParams(vmem_limit_bytes=50 * MIB),
        cost_estimate=pl.CostEstimate(
            flops=4 * rows * width * (cache_rows + rows),
            bytes_accessed=4 * (cache_rows + 2 * rows) * width,
            transcendentals=rows * heads * (cache_rows + rows),
        ),
        name="attention",
    )(jnp.stack([length, flip]), q, cache_keys, cache_values, new_keys, new_values)


def project_kernel(parts, order_ref, *refs):
    x_refs, w_refs = refs[:parts], refs[parts : 2 * parts]
    hidden_ref, gain_ref, resid_ref, normed_ref = refs[2 * parts :]
    g = pl.program_id(0)

    @pl.when(g == 0)
    def _():
        resid_ref[...] = hidden_ref[...].astype(jnp.float32)

    for x_ref, w_ref in zip(x_refs, w_refs):
        share = jnp.dot(x_ref[0], w_ref[0], preferred_element_type=jnp.float32)
        resid_ref[...] += share.astype(jnp.bfloat16).astype(jnp.float32)

    @pl.when(g == pl.num_programs(0) - 1)
    def _():
        normed_ref[...] = rms_scale(resid_ref[...], gain_ref[...]).astype(jnp.bfloat16)


def project_call(order, xs, weights, hidden, gain):
    parts = len(weights)
    steps, rows, width = xs[0].shape
    model = weights[0].shape[2]
    fixed = pl.BlockSpec((rows, model), lambda g, n: (0, 0))
    return pl.pallas_call(
        functools.partial(project_kernel, parts),
        grid_spec=pltpu.PrefetchScalarGridSpec(
            num_scalar_prefetch=1,
            grid=(steps,),
            in_specs=[pl.BlockSpec((1, rows, width), lambda g, n: (g, 0, 0))] * parts
            + [pl.BlockSpec((1, width, model), lambda g, n: (n[g], 0, 0))] * parts
            + [fixed, pl.BlockSpec((1, model), lambda g, n: (0, 0))],
            out_specs=[fixed, fixed],
        ),
        out_shape=[
            jax.ShapeDtypeStruct((rows, model), jnp.float32),
            jax.ShapeDtypeStruct((rows, model), jnp.bfloat16),
        ],
        compiler_params=pltpu.CompilerParams(vmem_limit_bytes=24 * MIB),
        cost_estimate=pl.CostEstimate(
            flops=2 * rows * model * steps * parts * width,
            bytes_accessed=2 * steps * parts * (width * model + rows * width) + 8 * rows * model,
            transcendentals=0,
        ),
        name="project",
    )(order, *xs, *weights, hidden, gain.reshape(1, model))


def share_kernel(order_ref, x_ref, w_ref, here_ref, beside_ref):
    tokens = here_ref.shape[0]
    x = x_ref[0].reshape(2 * tokens, x_ref.shape[3])
    share = jnp.dot(x, w_ref[0], preferred_element_type=jnp.float32)
    share = share.astype(jnp.bfloat16).astype(jnp.float32)

    @pl.when(pl.program_id(0) == 0)
    def _():
        here_ref[...] = share[:tokens]
        beside_ref[...] = share[tokens:]

    @pl.when(pl.program_id(0) > 0)
    def _():
        here_ref[...] += share[:tokens]
        beside_ref[...] += share[tokens:]


def share_call(order, x, weight):
    steps, unused, tokens, width = x.shape
    model = weight.shape[2]
    fixed = pl.BlockSpec((tokens, model), lambda g, n: (0, 0))
    return pl.pallas_call(
        share_kernel,
        grid_spec=pltpu.PrefetchScalarGridSpec(
            num_scalar_prefetch=1,
            grid=(steps,),
            in_specs=[
                pl.BlockSpec((1, 2, tokens, width), lambda g, n: (g, 0, 0, 0)),
                pl.BlockSpec((1, width, model), lambda g, n: (n[g], 0, 0)),
            ],
            out_specs=[fixed] * 2,
        ),
        out_shape=[jax.ShapeDtypeStruct((tokens, model), jnp.float32)] * 2,
        compiler_params=pltpu.CompilerParams(vmem_limit_bytes=24 * MIB),
        cost_estimate=pl.CostEstimate(
            flops=4 * tokens * model * steps * width,
            bytes_accessed=2 * steps * width * model + 8 * tokens * model,
            transcendentals=0,
        ),
        name="share",
    )(order, x, weight)


def norm_kernel(hidden_ref, here_ref, beside_ref, gain_ref, resid_ref, normed_ref):
    resid = hidden_ref[...].astype(jnp.float32) + here_ref[...] + beside_ref[...]
    resid_ref[...] = resid
    normed_ref[...] = rms_scale(resid, gain_ref[...]).astype(jnp.bfloat16)


def norm_call(hidden, here, beside, gain):
    return pl.pallas_call(
        norm_kernel,
        out_shape=[
            jax.ShapeDtypeStruct(hidden.shape, jnp.float32),
            jax.ShapeDtypeStruct(hidden.shape, jnp.bfloat16),
        ],
        compiler_params=pltpu.CompilerParams(vmem_limit_bytes=16 * MIB),
        cost_estimate=pl.CostEstimate(
            flops=8 * hidden.size, bytes_accessed=16 * hidden.size, transcendentals=0
        ),
        name="norm",
    )(hidden, here, beside, gain.reshape(1, -1))


def expert_kernel(half, counts, resident, *refs):
    x_refs = refs[: len(counts)]
    win_ref, wdown_ref = refs[len(counts) : len(counts) + 2]
    o_refs, acc_ref = refs[len(counts) + 2 : -1], refs[-1]
    h = pl.program_id(1)
    width = x_refs[0].shape[-1]
    x = [ref[...].reshape(-1, width) for ref in x_refs]
    x = x[0] if len(x) == 1 else jnp.concatenate(x, axis=0)
    at = pl.program_id(0) * pl.num_programs(1) + h if resident else 0
    both = jnp.dot(x, win_ref[at], preferred_element_type=jnp.float32)
    a = both[:, :half]
    b = both[:, half:]
    act = (a / (1.0 + jnp.exp(-a)) * b).astype(jnp.bfloat16)
    part = jnp.dot(act, wdown_ref[0], preferred_element_type=jnp.float32)

    @pl.when(h == 0)
    def _():
        acc_ref[...] = part

    @pl.when(h > 0)
    def _():
        acc_ref[...] += part

    @pl.when(h == pl.num_programs(1) - 1)
    def _():
        start = 0
        for ref in o_refs:
            size = ref.shape[0] * ref.shape[2]
            ref[...] = acc_ref[start : start + size].astype(jnp.bfloat16).reshape(ref.shape)
            start += size


def expert_call(xs, takes, outs, w_in, w_down, halves, resident=False):
    unused, unused, slots, width = xs[0].shape
    experts = w_in.shape[0] // halves
    units, model = w_down.shape[1:]
    rows = sum(takes) * slots
    block = lambda senders: pl.BlockSpec((senders, 1, slots, width), lambda e, h: (0, e, 0, 0))
    weight_specs = [
        pl.BlockSpec((1, width, 2 * units), lambda e, h: (e * halves + h, 0, 0)),
        pl.BlockSpec((1, units, model), lambda e, h: (e * halves + h, 0, 0)),
    ]
    if resident:
        weight_specs[0] = pl.BlockSpec(memory_space=pltpu.VMEM)
    return pl.pallas_call(
        functools.partial(expert_kernel, units, takes, resident),
        grid=(experts, halves),
        in_specs=[block(senders) for senders in takes] + weight_specs,
        out_specs=[block(senders) for senders in outs],
        out_shape=[
            jax.ShapeDtypeStruct((senders, experts, slots, width), jnp.bfloat16) for senders in outs
        ],
        scratch_shapes=[pltpu.VMEM((rows, model), jnp.float32)],
        compiler_params=pltpu.CompilerParams(vmem_limit_bytes=(24 if resident else 56) * MIB),
        cost_estimate=pl.CostEstimate(
            flops=6 * rows * experts * halves * width * units,
            bytes_accessed=2 * (w_in.size + w_down.size + 2 * rows * experts * width),
            transcendentals=rows * experts * halves * units,
        ),
        name="experts",
    )(*xs, w_in, w_down)


def xor_pairs(count, bits):
    return [(i, i ^ bits) for i in range(count)]


def gather_plane(block, later):
    rows = block.shape[0]
    along_x = lax.ppermute(block, "col", xor_pairs(8, 2))
    along_y = lax.ppermute(block, "col", xor_pairs(8, 4))
    along_x, along_y, later = lax.optimization_barrier((along_x, along_y, later))
    across_0 = lax.ppermute(along_x[: rows // 2], "col", xor_pairs(8, 4))
    across_1 = lax.ppermute(along_y[rows // 2 :], "col", xor_pairs(8, 2))
    mine = jnp.concatenate([block, along_x, along_y, across_0, across_1], axis=0)
    return mine, lax.ppermute(mine, "col", xor_pairs(8, 1)), later


def slot_places(ids, gates, experts):
    rows = ids.shape[-2]
    chosen = ids[..., None] == experts
    named = jnp.any(chosen, axis=-2)
    weight = jnp.sum(jnp.where(chosen, gates[..., None], 0.0), axis=-2)
    earlier = jnp.arange(rows)[:, None] > jnp.arange(rows)[None, :]
    rank = jnp.einsum(
        "ij,...je->...ie",
        earlier.astype(jnp.bfloat16),
        named.astype(jnp.bfloat16),
        preferred_element_type=jnp.float32,
    ).astype(jnp.int32)
    rank = jnp.where(named, rank, -1)
    place = rank[..., None] == jnp.arange(CAP, dtype=jnp.int32)
    gated = jnp.where(place, weight[..., None], 0.0).astype(jnp.bfloat16)
    flat = ids.shape[:-1] + (experts.shape[0] * CAP,)
    return place.reshape(flat).astype(jnp.bfloat16), gated.reshape(flat)


def route(place, rows):
    return lax.dot_general(
        place, rows, (((0,), (0,)), ((), ())), preferred_element_type=jnp.float32
    ).astype(jnp.bfloat16)


def experts_direct(moe_in, residual, expert_ids, gate_weights, w_in, w_down):
    tok_rows, model_width = moe_in.shape
    device_count = lax.axis_size("row") * lax.axis_size("col")
    place, place_gates = slot_places(
        expert_ids, gate_weights.astype(jnp.float32), jnp.arange(EXPERTS, dtype=jnp.int32)
    )
    per_device = w_in.shape[0]
    halves = 2 if per_device % 2 == 0 else 1
    copies = 2 // halves
    routed = route(place, moe_in).reshape(EXPERTS, 1, CAP, model_width)
    routed = jnp.broadcast_to(routed, (EXPERTS, copies, CAP, model_width))
    routed = routed.reshape(device_count, per_device // halves, CAP, model_width)
    received = lax.all_to_all(routed, ("row", "col"), split_axis=0, concat_axis=0, tiled=True)
    (parts,) = expert_call([received], [device_count], [device_count], w_in, w_down, halves)
    returned = lax.all_to_all(parts, ("row", "col"), split_axis=0, concat_axis=0, tiled=True)
    if copies > 1:
        returned = returned.reshape(EXPERTS, copies, CAP, model_width).astype(jnp.float32)
        returned = jnp.sum(returned, axis=1).astype(jnp.bfloat16)
    returned = returned.reshape(EXPERTS * CAP, model_width)
    expert_sum = jnp.dot(place_gates, returned, preferred_element_type=jnp.float32)
    return (residual + expert_sum).astype(jnp.bfloat16)


def plane_places(expert_ids, gate_weights):
    row, col = lax.axis_index("row"), lax.axis_index("col")
    packed = jnp.concatenate(
        [expert_ids.astype(jnp.float32), gate_weights.astype(jnp.float32)], axis=1
    )
    one, two, three = [lax.ppermute(packed, "row", xor_pairs(4, bits)) for bits in (1, 2, 3)]
    outer = (row == 0) | (row == 3)
    packed = jnp.stack(
        [packed, one, jnp.where(outer, two, three), jnp.where(outer, three, two)]
    )
    top = expert_ids.shape[1]
    device = row * 8 + (col ^ jnp.arange(8, dtype=jnp.int32))
    experts = (device[:, None] * 2 + jnp.arange(2, dtype=jnp.int32)).reshape(-1)
    return slot_places(packed[..., :top].astype(jnp.int32), packed[..., top:], experts)


def experts_planes(moe_in, residual, places, gated, w_in, w_down):
    model_width = moe_in.shape[1]
    swap, middle, outward = xor_pairs(4, 1), [(1, 2), (2, 1)], [(1, 0), (2, 3)]
    inward = [(0, 1), (3, 2)]
    near = lax.ppermute(moe_in, "row", swap)
    cross = lax.ppermute(moe_in, "row", middle)
    cross_out = lax.ppermute(cross, "row", outward)
    far = lax.ppermute(near, "row", middle)
    far_out = lax.ppermute(far, "row", outward)

    def send(routed):
        chips = [routed[:64]]
        chips += [
            lax.ppermute(routed[64 * r : 64 * (r + 1)], "col", xor_pairs(8, 2 * r))
            for r in range(1, 4)
        ]
        return chips

    def share(chips):
        return jnp.concatenate([chip[32:] for chip in chips], axis=0)

    def swap_cores(rows):
        return lax.ppermute(rows, "col", xor_pairs(8, 1))

    def views(chips, other):
        return [chip.reshape(2, 2, CAP, model_width) for chip in chips] + [
            other.reshape(4, 2, CAP, model_width)
        ]

    chips_0 = send(route(places[0], moe_in))
    routed_1 = route(places[1], near)
    shared_0, routed_1, cross = lax.optimization_barrier((share(chips_0), routed_1, cross))
    other_0 = swap_cores(shared_0)
    chips_1 = send(routed_1)
    routed_2 = route(places[2], cross + cross_out)
    shared_1, routed_2, far = lax.optimization_barrier((share(chips_1), routed_2, far))
    other_1 = swap_cores(shared_1)
    chips_2 = send(routed_2)
    routed_3 = route(places[3], far + far_out)
    shared_2, routed_3 = lax.optimization_barrier((share(chips_2), routed_3))
    other_2 = swap_cores(shared_2)
    chips_3 = send(routed_3)
    other_3 = swap_cores(share(chips_3))

    def expert_parts(*blocks):
        xs = [view for chips, other in blocks for view in views(chips, other)]
        takes, outs = [1, 1, 1, 1, 4] * len(blocks), [4, 4] * len(blocks)
        return expert_call(xs, takes, outs, w_in, w_down, 2)

    parts = expert_parts(
        (chips_0, other_0), (chips_1, other_1), (chips_2, other_2), (chips_3, other_3)
    )

    def give_back(own, other, before=None):
        both = [
            jnp.concatenate([own[r].reshape(32, model_width), other[r].reshape(32, model_width)])
            for r in range(4)
        ]
        if before is not None:
            *both, unused = lax.optimization_barrier((*both, before[1]))
        return both[:1] + [
            lax.ppermute(both[r], "col", xor_pairs(8, 2 * r)) for r in range(1, 4)
        ]

    def combine(gates, chips):
        total = jnp.dot(gates[:, :64], chips[0], preferred_element_type=jnp.float32)
        for r in range(1, 4):
            total += jnp.dot(
                gates[:, 64 * r : 64 * (r + 1)], chips[r], preferred_element_type=jnp.float32
            )
        return total

    def narrow(total):
        return total.astype(jnp.bfloat16)

    back_2 = give_back(parts[4], swap_cores(parts[5]))
    back_3 = give_back(parts[6], swap_cores(parts[7]), back_2)
    sum_2 = combine(gated[2], back_2)
    hop = lax.ppermute(narrow(sum_2), "row", inward)
    back_1 = give_back(parts[2], swap_cores(parts[3]), back_3)
    sum_3 = narrow(combine(gated[3], back_3))
    ends = lax.ppermute(sum_3, "row", [(0, 3), (3, 0)])
    inner = lax.ppermute(sum_3, "row", [(1, 3), (2, 0)])
    back_0 = give_back(parts[0], swap_cores(parts[1]), back_1)
    middles = lax.ppermute(narrow(sum_2 + hop.astype(jnp.float32)), "row", middle)
    beside = lax.ppermute(narrow(combine(gated[1], back_1)), "row", swap)
    total = residual + combine(gated[0], back_0)
    for arrived in (ends, inner, beside, middles):
        total += arrived.astype(jnp.float32)
    return total.astype(jnp.bfloat16)


def body(
    hidden,
    cached_lengths,
    request_order,
    cache_keys,
    cache_values,
    attn_gain,
    w_qkv,
    w_out,
    moe_gain,
    expert_ids,
    gate_weights,
    w_in,
    w_down,
):
    tok_rows, model_width = hidden.shape
    heads_here = w_qkv.shape[1]
    row_count = lax.axis_size("row")
    col_count = lax.axis_size("col")
    device_count = row_count * col_count
    new_rows = tok_rows * col_count

    planes = row_count == 4 and col_count == 8 and w_in.shape[0] == 4

    row_index = lax.axis_index("row")
    places = jnp.arange(request_order.shape[0], dtype=jnp.int32)
    request = jnp.sum(jnp.where(places == row_index, request_order, 0))
    length = jnp.sum(jnp.where(places == request, cached_lengths, 0))
    query_pos = length + jnp.arange(new_rows, dtype=jnp.int32)
    frequency = THETA ** (-2.0 * jnp.arange(HEAD // 2, dtype=jnp.float32) / HEAD)
    angles = query_pos.astype(jnp.float32)[:, None] * frequency
    cosine, sine = jnp.cos(angles), jnp.sin(angles)
    cosine = jnp.concatenate([cosine, cosine], axis=1)
    sine = jnp.concatenate([-sine, sine], axis=1)

    w_matrix = w_qkv.reshape(model_width, -1)
    normed = rms_scale(hidden, attn_gain).astype(jnp.bfloat16)
    if planes:
        col = lax.axis_index("col")
        chips = jnp.arange(4, dtype=jnp.int32)
        slots, gated = plane_places(expert_ids, gate_weights)
        mine, other, w_out_late = gather_plane(normed, w_out)
        even_odd = [[0, 2, 4, 6], [1, 3, 5, 7]]
        w_out_mine = lax.all_gather(w_out_late, "col", axis=0, axis_index_groups=even_odd)
        fresh = qkv_call(col ^ 2 * chips, mine, w_matrix, cosine, sine, heads_here)
        queries, new_keys, new_values = qkv_call(
            col ^ 2 * chips ^ 1, other, w_matrix, cosine, sine, heads_here, fresh
        )
        context = attention_call(
            length, col, tok_rows, queries, cache_keys, cache_values, new_keys, new_values
        )
        arrived = [context[:2]] + [
            lax.ppermute(context[2 * r : 2 * r + 2], "col", xor_pairs(8, 2 * r))
            for r in range(1, 4)
        ]
        here, beside = share_call((col >> 1) ^ chips, jnp.stack(arrived), w_out_mine)
        beside = lax.ppermute(beside, "col", xor_pairs(8, 1))
        residual, moe_in = norm_call(hidden, here, beside, moe_gain)
        new_hidden = experts_planes(moe_in, residual, slots, gated, w_in, w_down)
    else:
        gathered = lax.all_gather(normed, "col", axis=0, tiled=True)
        w_out_all = lax.all_gather(w_out, "col", axis=0)
        blocks = jnp.arange(col_count, dtype=jnp.int32)
        queries, new_keys, new_values = qkv_call(
            blocks, gathered, w_matrix, cosine, sine, heads_here
        )
        context = attention_call(
            length,
            jnp.int32(0),
            tok_rows,
            queries,
            cache_keys,
            cache_values,
            new_keys,
            new_values,
        )
        shares = lax.all_to_all(context, "col", 0, 0, tiled=True)
        residual, moe_in = project_call(blocks, [shares], [w_out_all], hidden, moe_gain)
        new_hidden = experts_direct(moe_in, residual, expert_ids, gate_weights, w_in, w_down)
    return (new_hidden, new_keys, new_values)


def solution(mesh):
    in_specs = (
        P(("row", "col"), None),
        P(),
        P(),
        P("row", None, "col"),
        P("row", None, "col"),
        P(),
        P(None, "col", None),
        P("col", None),
        P(),
        P(("row", "col"), None),
        P(("row", "col"), None),
        P(("row", "col"), None, None),
        P(("row", "col"), None, None),
    )
    out_specs = (P(("row", "col"), None), P("row", "col"), P("row", "col"))
    return jax.shard_map(body, mesh=mesh, in_specs=in_specs, out_specs=out_specs, check_vma=False)
```
